512 devices in a mesh: ctx: 64 (over x, y, core), head: 8 (over z).
Axes of the slice: x: 4, y: 8, z: 8, core: 2. Of those that a mesh axis runs over, the one named last changes fastest.
Arguments:
- queries: bfloat16 [512, 8192], P('ctx', 'head'), may hold values from -128 to 128
- fresh_span_keys: bfloat16 [512, 1024], P('ctx', 'head'), may hold values from -10 to 10
- fresh_span_values: bfloat16 [512, 1024], P('ctx', 'head'), may hold values from -6 to 6
- context_keys: bfloat16 [262144, 1024], P('ctx', 'head'), may hold values from -6 to 6
- context_values: bfloat16 [262144, 1024], P('ctx', 'head'), may hold values from -12 to 12
- selected: int32 [4, 12], replicated, may hold values from 0 to 63, as said below
- out_weight: bfloat16 [8192, 8192], P('head', 'ctx'), may hold values from -0.0625 to 0.0625
Outputs:
- attended: bfloat16 [512, 8192], P('head', 'ctx')
The draws below stay inside these ranges and needn't reach their ends.
Inputs may be any that keep to these rules, and one draw needn't show every extreme that they name: `selected`: each row lists 12 different cache blocks, and every row lists the newest block, 63.
All inputs are finite; a program needn't handle non-finite values.
Results may differ from the reference program's by a relative error of at most 0.01345.
Values may be sent and summed in bfloat16 or wider, within the bound.
A program may use at most 64 MiB of HBM per device.

```python
import jax
import jax.numpy as jnp
from jax import lax

D = 8192
QUERY_HEADS = 64
KEY_VALUE_HEADS = 8
HEAD_SIZE = 128
GROUP_QUERIES = 8
BLOCK_TOKENS = 4096
QUERY_BLOCK_SIZE = 128
PICKED_BLOCKS = 12
SPAN_TOKENS = 512
QUERY_BLOCKS = 4
CACHE_BLOCKS = 64
CACHED_TOKENS = 262144


def span_pair(key):
    base = jax.random.fold_in(key, 7301)
    query_seed, span_seed = jax.random.split(base, 2)
    key_matrix = 1.6 * jnp.clip(jax.random.normal(span_seed, (SPAN_TOKENS, KEY_VALUE_HEADS, HEAD_SIZE), jnp.float32), -6.0, 6.0)
    query_matrix = 2.0 * jnp.clip(jax.random.normal(query_seed, (SPAN_TOKENS, KEY_VALUE_HEADS, GROUP_QUERIES, HEAD_SIZE), jnp.float32), -6.0, 6.0)
    return (query_matrix.reshape(SPAN_TOKENS, QUERY_HEADS * HEAD_SIZE), key_matrix.reshape(SPAN_TOKENS, KEY_VALUE_HEADS * HEAD_SIZE))


def draw_queries(key, part):
    return span_pair(key)[0].astype(jnp.bfloat16)


def draw_fresh_span_keys(key, part):
    return span_pair(key)[1].astype(jnp.bfloat16)


def draw_context_values(key, part):
    base = jax.random.fold_in(key, 4409)
    average_key, random_seed_key = jax.random.split(base, 2)
    block_averages = jnp.clip(jax.random.normal(average_key, (CACHE_BLOCKS, 1, KEY_VALUE_HEADS * HEAD_SIZE), jnp.float32), -4.0, 4.0)
    random_draws = jnp.clip(jax.random.normal(random_seed_key, (CACHE_BLOCKS, BLOCK_TOKENS, KEY_VALUE_HEADS * HEAD_SIZE), jnp.float32), -6.0, 6.0)
    return (block_averages + random_draws).reshape(CACHE_BLOCKS * BLOCK_TOKENS, KEY_VALUE_HEADS * HEAD_SIZE).astype(jnp.bfloat16)


def draw_selected(key, part):
    score_key = jax.random.fold_in(key, 9127)
    base = jax.random.randint(score_key, (QUERY_BLOCKS, CACHE_BLOCKS), 0, 1 << 20, dtype=jnp.int32)
    block_ids = jnp.arange(CACHE_BLOCKS, dtype=jnp.int32)
    ranked = base * CACHE_BLOCKS + block_ids[None, :]
    ranked = jnp.where(block_ids[None, :] == CACHE_BLOCKS - 1, jnp.int32(1 << 30), ranked)
    return lax.top_k(ranked, PICKED_BLOCKS)[1].astype(jnp.int32)


def block_levels(own_key, dims, cuts, low, largest):
    factor_of, own = 1.0, jax.random.fold_in(own_key, 6)
    for axis_at, blocks in cuts:
        draws = jnp.exp(jax.random.uniform(jax.random.fold_in(own, axis_at), (blocks,), jnp.float32, low / len(cuts), largest / len(cuts)))
        factor_of = factor_of * jnp.repeat(draws, dims[axis_at] // blocks).reshape([-1 if axis == axis_at else 1 for axis in range(len(dims))])
    return factor_of


def noise(rng, shape, spread, reach, pieces=(), held_as=jnp.bfloat16):
    level = block_levels(rng, shape, pieces, -0.22, 0.18) if pieces else 1.0
    result = jax.random.normal(rng, shape, jnp.float32) * spread * level
    return jnp.minimum(jnp.maximum(result, -reach), reach).astype(held_as)


def setup_inputs(seed: int = 0) -> dict:
    seeds = jax.random.split(jax.random.key(seed), 8)
    queries = draw_queries(jax.random.fold_in(seeds[7], 71), 0)
    fresh_span_keys = draw_fresh_span_keys(jax.random.fold_in(seeds[7], 71), 0)
    fresh_span_values = noise(seeds[2], (SPAN_TOKENS, KEY_VALUE_HEADS * HEAD_SIZE), 1.0, 6.0, ((0, 64), (1, 8)))
    context_keys = noise(seeds[3], (CACHED_TOKENS, KEY_VALUE_HEADS * HEAD_SIZE), 1.0, 6.0, ((0, 64), (1, 8)))
    context_values = draw_context_values(jax.random.fold_in(seeds[7], 71), 0)
    selected = draw_selected(jax.random.fold_in(seeds[7], 71), 0)
    out_weight = noise(seeds[6], (QUERY_HEADS * HEAD_SIZE, D), (QUERY_HEADS * HEAD_SIZE) ** -0.5, 0.0625, ((0, 8), (1, 64)))
    return {"queries": queries, "fresh_span_keys": fresh_span_keys, "fresh_span_values": fresh_span_values, "context_keys": context_keys, "context_values": context_values, "selected": selected, "out_weight": out_weight}


def reference(queries, fresh_span_keys, fresh_span_values, context_keys, context_values, selected, out_weight):
    score_scale = HEAD_SIZE ** -0.5
    keys_by_block = context_keys.reshape(CACHE_BLOCKS, BLOCK_TOKENS, KEY_VALUE_HEADS, HEAD_SIZE)
    values_by_block = context_values.reshape(CACHE_BLOCKS, BLOCK_TOKENS, KEY_VALUE_HEADS, HEAD_SIZE)
    keys_of_span = fresh_span_keys.reshape(SPAN_TOKENS, KEY_VALUE_HEADS, HEAD_SIZE)
    values_of_span = fresh_span_values.reshape(SPAN_TOKENS, KEY_VALUE_HEADS, HEAD_SIZE)
    query_groups = queries.reshape(QUERY_BLOCKS, QUERY_BLOCK_SIZE, KEY_VALUE_HEADS, GROUP_QUERIES, HEAD_SIZE)
    key_pos = jnp.arange(SPAN_TOKENS, dtype=jnp.int32)

    def one_block(block_index):
        picked_blocks = lax.dynamic_index_in_dim(selected, block_index, 0, keepdims=False)
        joined_keys = jnp.concatenate([jnp.take(keys_by_block, picked_blocks, axis=0).reshape(PICKED_BLOCKS * BLOCK_TOKENS, KEY_VALUE_HEADS, HEAD_SIZE), keys_of_span], axis=0)
        joined_values = jnp.concatenate([jnp.take(values_by_block, picked_blocks, axis=0).reshape(PICKED_BLOCKS * BLOCK_TOKENS, KEY_VALUE_HEADS, HEAD_SIZE), values_of_span], axis=0)
        row_pos = block_index * QUERY_BLOCK_SIZE + jnp.arange(QUERY_BLOCK_SIZE, dtype=jnp.int32)
        causal = key_pos[None, :] <= row_pos[:, None]
        valid_mask = jnp.concatenate([jnp.ones((QUERY_BLOCK_SIZE, PICKED_BLOCKS * BLOCK_TOKENS), jnp.bool_), causal], axis=1)
        block_queries = lax.dynamic_index_in_dim(query_groups, block_index, 0, keepdims=False)

        def single_head(head_index):
            query_matrix = lax.dynamic_index_in_dim(block_queries, head_index, 1, keepdims=False).reshape(QUERY_BLOCK_SIZE * GROUP_QUERIES, HEAD_SIZE)
            head_keys = lax.dynamic_index_in_dim(joined_keys, head_index, 1, keepdims=False)
            head_values = lax.dynamic_index_in_dim(joined_values, head_index, 1, keepdims=False)
            scores = lax.dot_general(query_matrix, head_keys, (((1,), (1,)), ((), ())), preferred_element_type=jnp.float32) * score_scale
            scores = scores.reshape(QUERY_BLOCK_SIZE, GROUP_QUERIES, -1)
            scores = jnp.where(valid_mask[:, None, :], scores, -jnp.inf)
            weights = jnp.exp(scores - jnp.max(scores, axis=-1, keepdims=True))
            denominator = jnp.sum(weights, axis=-1)
            summed = jnp.dot(weights.astype(jnp.bfloat16).reshape(QUERY_BLOCK_SIZE * GROUP_QUERIES, -1), head_values, preferred_element_type=jnp.float32)
            return summed.reshape(QUERY_BLOCK_SIZE, GROUP_QUERIES, HEAD_SIZE) / denominator[..., None]

        output_per_head = lax.map(single_head, jnp.arange(KEY_VALUE_HEADS, dtype=jnp.int32))
        return jnp.transpose(output_per_head, (1, 0, 2, 3)).reshape(QUERY_BLOCK_SIZE, QUERY_HEADS * HEAD_SIZE)

    attention = lax.map(one_block, jnp.arange(QUERY_BLOCKS, dtype=jnp.int32)).reshape(SPAN_TOKENS, QUERY_HEADS * HEAD_SIZE).astype(jnp.bfloat16)
    return jnp.dot(attention, out_weight, preferred_element_type=jnp.float32).astype(jnp.bfloat16)
```

```python
import math

import jax
import jax.numpy as jnp
from jax import lax
from jax.experimental import pallas as pl
from jax.experimental.pallas import tpu as pltpu
from jax.sharding import PartitionSpec as P

HEAD_SIZE = 128
BLOCK_TOKENS = 4096
QUERY_BLOCK = 128
QUERY_BLOCKS = 4
PICKED = 12
SPAN = 512
NX, NY, NZ = 4, 8, 8
CORE_HEADS = 4
HALF = CORE_HEADS * HEAD_SIZE
WIDE = HALF + HEAD_SIZE
CHIP_TOKENS = 16
ROWS = CORE_HEADS * QUERY_BLOCK
KEY_PIECE = 1024

EXP2_SCALE = math.log2(math.e) / math.sqrt(HEAD_SIZE)
NEG = -(2.0**100)
NEAR_FIRST = (1, 7, 2, 6, 3, 5, 4)
MESH = pl.DeviceIdType.MESH


def place():
    me = lax.axis_index("ctx")
    core = lax.rem(me, 2)
    chip = me // 2
    return me, chip // NY, lax.rem(chip, NY), core, lax.axis_index("head")


def greet(ids):
    barrier = pltpu.get_barrier_semaphore()
    for device in ids:
        pl.semaphore_signal(barrier, inc=1, device_id=device, device_id_type=MESH)
    pl.semaphore_wait(barrier, len(ids))


def remote(src, dst, send, recv, device):
    return pltpu.make_async_remote_copy(
        src_ref=src,
        dst_ref=dst,
        send_sem=send,
        recv_sem=recv,
        device_id=device,
        device_id_type=MESH,
    )


def gather_kernel(
    q_ref,
    fk_ref,
    fv_ref,
    ck_ref,
    cv_ref,
    qall_ref,
    sk_ref,
    sv_ref,
    pk_ref,
    pv_ref,
    own_sem,
    pair_send,
    pair_recv,
    y_send,
    y_recv,
    x_send,
    x_recv,
):
    me, x, y, core, z = place()
    chip = me // 2
    other = me + 1 - 2 * core

    def device(dx, dy):
        return ((lax.rem(x + dx, NX) * NY + lax.rem(y + dy, NY)) * 2 + core, z)

    def chunk(dx, dy):
        row = lax.rem(x + NX - dx, NX) * NY + lax.rem(y + NY - dy, NY)
        return qall_ref.at[pl.ds(row * 2, 2)]

    greet(
        [(other, z)]
        + [device(0, dy) for dy in range(1, NY)]
        + [device(dx, 0) for dx in range(1, NX)]
    )

    own_half = q_ref.at[:, pl.ds(pl.multiple_of(core * HALF, HALF), HALF)]
    other_half = q_ref.at[:, pl.ds(pl.multiple_of((1 - core) * HALF, HALF), HALF)]
    pairs = [
        remote(src, dst, pair_send.at[n], pair_recv.at[n], (other, z))
        for n, (src, dst) in enumerate(
            (
                (other_half, qall_ref.at[me]),
                (fk_ref, sk_ref.at[core]),
                (fv_ref, sv_ref.at[core]),
                (ck_ref, pk_ref),
                (cv_ref, pv_ref),
            )
        )
    ]
    owns = [
        pltpu.make_async_copy(src, dst, own_sem.at[n])
        for n, (src, dst) in enumerate(
            (
                (own_half, qall_ref.at[me]),
                (fk_ref, sk_ref.at[core]),
                (fv_ref, sv_ref.at[core]),
            )
        )
    ]
    pairs[0].start()
    for copy in owns:
        copy.start()
    for copy in pairs[1:]:
        copy.start()
    owns[0].wait()
    remote(
        other_half, qall_ref.at[other], pair_send.at[0], pair_recv.at[0], (other, z)
    ).wait_recv()

    sends = []

    def along_y(dy):
        copy = remote(chunk(0, 0), chunk(0, 0), y_send.at[dy], y_recv.at[dy], device(0, dy))
        copy.start()
        sends.append(copy)

    def along_x(dx, dy):
        copy = remote(
            chunk(0, dy), chunk(0, dy), x_send.at[dx, dy], x_recv.at[dx, dy], device(dx, 0)
        )
        copy.start()
        sends.append(copy)

    for dy in (4, 3, 5, 2, 6, 1, 7):
        along_y(dy)
    for dx in (2, 1, 3):
        along_x(dx, 0)
    for dy in NEAR_FIRST:
        remote(
            chunk(0, dy), chunk(0, dy), y_send.at[dy], y_recv.at[dy], device(0, dy)
        ).wait_recv()
        for dx in (2, 1, 3):
            along_x(dx, dy)
    for dy in (0,) + NEAR_FIRST:
        for dx in (1, 3, 2):
            remote(
                chunk(dx, dy), chunk(dx, dy), x_send.at[dx, dy], x_recv.at[dx, dy], device(dx, 0)
            ).wait_recv()
    for copy in sends:
        copy.wait_send()
    for copy in owns[1:]:
        copy.wait()
    pairs[0].wait_send()
    spots = (sk_ref.at[1 - core], sv_ref.at[1 - core], pk_ref, pv_ref)
    for n, copy in enumerate(pairs[1:]):
        copy.wait_send()
        remote(
            spots[n], spots[n], pair_send.at[n + 1], pair_recv.at[n + 1], (other, z)
        ).wait_recv()


def gather(queries, fresh_keys, fresh_values, cache_keys, cache_values):
    anywhere = pl.BlockSpec(memory_space=pl.ANY)
    bf16 = jnp.bfloat16
    dma = pltpu.SemaphoreType.DMA
    return pl.pallas_call(
        gather_kernel,
        out_shape=(
            jax.ShapeDtypeStruct((2 * NX * NY, 8, HALF), bf16),
            jax.ShapeDtypeStruct((2, 8, HEAD_SIZE), bf16),
            jax.ShapeDtypeStruct((2, 8, HEAD_SIZE), bf16),
            jax.ShapeDtypeStruct((BLOCK_TOKENS, HEAD_SIZE), bf16),
            jax.ShapeDtypeStruct((BLOCK_TOKENS, HEAD_SIZE), bf16),
        ),
        in_specs=[anywhere] * 5,
        out_specs=[anywhere] * 5,
        scratch_shapes=[
            dma((3,)),
            dma((5,)),
            dma((5,)),
            dma((NY,)),
            dma((NY,)),
            dma((NX, NY)),
            dma((NX, NY)),
        ],
        compiler_params=pltpu.CompilerParams(collective_id=0, has_side_effects=True),
        name="gather_spans",
    )(queries, fresh_keys, fresh_values, cache_keys, cache_values)


def attend_kernel(
    sel_ref,
    q_ref,
    sk_ref,
    sv_ref,
    ck_ref,
    cv_ref,
    pk_ref,
    pv_ref,
    out_ref,
    kbuf,
    vbuf,
    qs,
    m_s,
    l_s,
    acc_s,
    sems,
):
    me, x, y, core, z = place()
    chip = me // 2
    copies = [
        pltpu.make_async_copy(src, dst, sems.at[n])
        for n, (src, dst) in enumerate(
            (
                (ck_ref, kbuf.at[0]),
                (cv_ref, vbuf.at[0]),
                (pk_ref, kbuf.at[1]),
                (pv_ref, vbuf.at[1]),
            )
        )
    ]
    for copy in copies:
        copy.start()

    lane = lax.broadcasted_iota(jnp.int32, (ROWS, HEAD_SIZE), 1)
    stat_lane = lax.broadcasted_iota(jnp.int32, (QUERY_BLOCK, HEAD_SIZE), 1)

    @pl.loop(0, QUERY_BLOCKS)
    def _(j):
        start = pl.multiple_of(j * QUERY_BLOCK, QUERY_BLOCK)
        for g in range(CORE_HEADS):
            qs[g * QUERY_BLOCK : (g + 1) * QUERY_BLOCK] = q_ref[
                pl.ds(start, QUERY_BLOCK), g * HEAD_SIZE : (g + 1) * HEAD_SIZE
            ]
        s = lax.dot_general(
            qs[...], sk_ref[...], (((1,), (1,)), ((), ())), preferred_element_type=jnp.float32
        )
        token = j * QUERY_BLOCK + lax.rem(
            lax.broadcasted_iota(jnp.int32, s.shape, 0), QUERY_BLOCK
        )
        key = chip * CHIP_TOKENS + lax.broadcasted_iota(jnp.int32, s.shape, 1)
        keep = key <= token
        s = jnp.where(keep, s, NEG)
        m = jnp.max(s, axis=1, keepdims=True)
        p = jnp.where(keep, jnp.exp2((s - m) * EXP2_SCALE), 0.0)
        m_s[...] = jnp.broadcast_to(m, m_s.shape)
        l_s[...] = jnp.where(lane == 0, jnp.sum(p, axis=1, keepdims=True), 0.0)
        acc_s[...] = jnp.dot(
            p.astype(jnp.bfloat16), sv_ref[...], preferred_element_type=jnp.float32
        )

        @pl.when(j == 0)
        def _():
            for copy in copies:
                copy.wait()

        for b in range(2):
            block = me if b == 0 else me + 1 - 2 * core
            wanted = sel_ref[j, 0] == block
            for n in range(1, PICKED):
                wanted = jnp.logical_or(wanted, sel_ref[j, n] == block)

            @pl.when(wanted)
            def _():
                @pl.loop(0, BLOCK_TOKENS // KEY_PIECE)
                def _(n):
                    rows = pl.ds(pl.multiple_of(n * KEY_PIECE, KEY_PIECE), KEY_PIECE)
                    keys = kbuf[b, rows, :]
                    values = vbuf[b, rows, :]
                    scores = lax.dot_general(
                        qs[...], keys, (((1,), (1,)), ((), ())), preferred_element_type=jnp.float32
                    )
                    m_old = m_s[...]
                    m_new = jnp.maximum(m_old, jnp.max(scores, axis=1, keepdims=True))
                    shrink = jnp.exp2((m_old - m_new) * EXP2_SCALE)
                    m_s[...] = m_new
                    parts = []
                    total = l_s[...] * shrink
                    for t in range(KEY_PIECE // HEAD_SIZE):
                        part = jnp.exp2(
                            (scores[:, t * HEAD_SIZE : (t + 1) * HEAD_SIZE] - m_new) * EXP2_SCALE
                        )
                        total = total + part
                        parts.append(part.astype(jnp.bfloat16))
                    l_s[...] = total
                    acc_s[...] = acc_s[...] * shrink + jnp.dot(
                        jnp.concatenate(parts, axis=1), values, preferred_element_type=jnp.float32
                    )

        m = m_s[...]
        m_sent = m.astype(jnp.bfloat16).astype(jnp.float32)
        grow = jnp.exp2((m - m_sent) * EXP2_SCALE)
        total = jnp.sum(l_s[...], axis=1, keepdims=True) * grow
        high = total.astype(jnp.bfloat16).astype(jnp.float32)
        low = total - high
        acc = acc_s[...] * grow
        stats = jnp.zeros((QUERY_BLOCK, HEAD_SIZE), jnp.float32)
        for g in range(CORE_HEADS):
            here = slice(g * QUERY_BLOCK, (g + 1) * QUERY_BLOCK)
            out_ref[j, :, g * HEAD_SIZE : (g + 1) * HEAD_SIZE] = acc[here].astype(jnp.bfloat16)
            stats = jnp.where(stat_lane == g, m_sent[here], stats)
            stats = jnp.where(stat_lane == CORE_HEADS + g, high[here], stats)
            stats = jnp.where(stat_lane == 2 * CORE_HEADS + g, low[here], stats)
        out_ref[j, :, HALF:WIDE] = stats.astype(jnp.bfloat16)


def attend(selected, q_all, span_keys, span_values, own_k, own_v, pair_k, pair_v):
    anywhere = pl.BlockSpec(memory_space=pl.ANY)
    vmem = pl.BlockSpec(memory_space=pltpu.VMEM)
    f32 = jnp.float32
    return pl.pallas_call(
        attend_kernel,
        out_shape=jax.ShapeDtypeStruct((QUERY_BLOCKS, QUERY_BLOCK, WIDE), jnp.bfloat16),
        in_specs=[pl.BlockSpec(memory_space=pltpu.SMEM), vmem, vmem, vmem] + [anywhere] * 4,
        out_specs=vmem,
        scratch_shapes=[
            pltpu.VMEM((2, BLOCK_TOKENS, HEAD_SIZE), jnp.bfloat16),
            pltpu.VMEM((2, BLOCK_TOKENS, HEAD_SIZE), jnp.bfloat16),
            pltpu.VMEM((ROWS, HEAD_SIZE), jnp.bfloat16),
            pltpu.VMEM((ROWS, HEAD_SIZE), f32),
            pltpu.VMEM((ROWS, HEAD_SIZE), f32),
            pltpu.VMEM((ROWS, HEAD_SIZE), f32),
            pltpu.SemaphoreType.DMA((4,)),
        ],
        name="attend_blocks",
    )(selected, q_all, span_keys, span_values, own_k, own_v, pair_k, pair_v)


def merge(pieces):
    stats = [piece[:, HALF:WIDE].astype(jnp.float32) for piece in pieces]
    joined = []
    for g in range(CORE_HEADS):
        tops = [stat[:, g : g + 1] for stat in stats]
        top = tops[0]
        for one in tops[1:]:
            top = jnp.maximum(top, one)
        total = jnp.zeros_like(top)
        acc = None
        for piece, stat, one in zip(pieces, stats, tops):
            weight = jnp.exp2((one - top) * EXP2_SCALE)
            total = total + weight * (
                stat[:, CORE_HEADS + g : CORE_HEADS + g + 1]
                + stat[:, 2 * CORE_HEADS + g : 2 * CORE_HEADS + g + 1]
            )
            term = weight * piece[:, g * HEAD_SIZE : (g + 1) * HEAD_SIZE].astype(jnp.float32)
            acc = term if acc is None else acc + term
        joined.append((top, total, acc))
    return joined


def combine_kernel(
    part_ref,
    w_ref,
    out_ref,
    own,
    from_x,
    merged,
    from_y,
    rows,
    partial,
    from_z,
    own_sem,
    x_send,
    x_recv,
    y_send,
    y_recv,
    ay_send,
    ay_recv,
    ax_send,
    ax_recv,
    c_send,
    c_recv,
    z_send,
    z_recv,
):
    me, x, y, core, z = place()
    other = me + 1 - 2 * core
    f32 = jnp.float32

    def device(dx, dy):
        return ((lax.rem(x + dx, NX) * NY + lax.rem(y + dy, NY)) * 2 + core, z)

    greet(
        [(other, z)]
        + [device(0, dy) for dy in range(1, NY)]
        + [device(dx, 0) for dx in range(1, NX)]
        + [(me, lax.rem(z + dz, NZ)) for dz in range(1, NZ)]
    )
    sends = []

    for dx in (2, 1, 3):
        copy = remote(
            part_ref.at[lax.rem(x + dx, NX)],
            from_x.at[dx],
            x_send.at[dx],
            x_recv.at[dx],
            device(dx, 0),
        )
        copy.start()
        sends.append(copy)
    mine = pltpu.make_async_copy(part_ref.at[x], own, own_sem)
    mine.start()
    mine.wait()
    for dx in range(1, NX):
        remote(
            from_x.at[dx], from_x.at[dx], x_send.at[dx], x_recv.at[dx], device(dx, 0)
        ).wait_recv()

    stat_lane = lax.broadcasted_iota(jnp.int32, (CHIP_TOKENS, HEAD_SIZE), 1)

    @pl.loop(1, NY + 1)
    def _(dy):
        at = lax.rem(y + dy, NY)
        here = pl.ds(pl.multiple_of(at * CHIP_TOKENS, CHIP_TOKENS), CHIP_TOKENS)
        joined = merge([own[here, :]] + [from_x[dx, here, :] for dx in range(1, NX)])
        stats = jnp.zeros((CHIP_TOKENS, HEAD_SIZE), f32)
        for g, (top, total, acc) in enumerate(joined):
            high = total.astype(jnp.bfloat16).astype(f32)
            stats = jnp.where(stat_lane == g, top, stats)
            stats = jnp.where(stat_lane == CORE_HEADS + g, high, stats)
            stats = jnp.where(stat_lane == 2 * CORE_HEADS + g, total - high, stats)
            merged[at, :, g * HEAD_SIZE : (g + 1) * HEAD_SIZE] = acc.astype(jnp.bfloat16)
        merged[at, :, HALF:WIDE] = stats.astype(jnp.bfloat16)

    for dy in (4, 3, 5, 2, 6, 1, 7):
        copy = remote(
            merged.at[lax.rem(y + dy, NY)],
            from_y.at[dy],
            y_send.at[dy],
            y_recv.at[dy],
            device(0, dy),
        )
        copy.start()
        sends.append(copy)
    for dy in range(1, NY):
        remote(
            from_y.at[dy], from_y.at[dy], y_send.at[dy], y_recv.at[dy], device(0, dy)
        ).wait_recv()
    joined = merge([merged[y]] + [from_y[dy] for dy in range(1, NY)])
    for g, (_, total, acc) in enumerate(joined):
        rows[x, core, y, :, g * HEAD_SIZE : (g + 1) * HEAD_SIZE] = (acc / total).astype(
            jnp.bfloat16
        )

    def spot(dx, dy):
        return rows.at[lax.rem(x + NX - dx, NX), core, lax.rem(y + NY - dy, NY)]

    for dy in (4, 3, 5, 2, 6, 1, 7):
        copy = remote(spot(0, 0), spot(0, 0), ay_send.at[dy], ay_recv.at[dy], device(0, dy))
        copy.start()
        sends.append(copy)
    for dy in (0,) + NEAR_FIRST:
        if dy:
            remote(
                spot(0, dy), spot(0, dy), ay_send.at[dy], ay_recv.at[dy], device(0, dy)
            ).wait_recv()
        for dx in (2, 1, 3):
            copy = remote(
                spot(0, dy), spot(0, dy), ax_send.at[dx, dy], ax_recv.at[dx, dy], device(dx, 0)
            )
            copy.start()
            sends.append(copy)
    for dx in (0, 1, 3, 2):
        if dx:
            for dy in (0,) + NEAR_FIRST:
                remote(
                    spot(dx, dy), spot(dx, dy), ax_send.at[dx, dy], ax_recv.at[dx, dy], device(dx, 0)
                ).wait_recv()
        at = lax.rem(x + NX - dx, NX)
        copy = remote(
            rows.at[at, core], rows.at[at, core], c_send.at[dx], c_recv.at[dx], (other, z)
        )
        copy.start()
        sends.append(copy)
        remote(
            rows.at[at, 1 - core], rows.at[at, 1 - core], c_send.at[dx], c_recv.at[dx], (other, z)
        ).wait_recv()
        product = jnp.dot(
            rows[at, 0].reshape(QUERY_BLOCK, HALF), w_ref[:HALF, :], preferred_element_type=f32
        ) + jnp.dot(
            rows[at, 1].reshape(QUERY_BLOCK, HALF), w_ref[HALF:, :], preferred_element_type=f32
        )
        product = product.astype(jnp.bfloat16)
        for half in range(2):
            to = 2 * at + half
            partial[to] = product[half * 64 : (half + 1) * 64]
        for half in range(2):
            to = 2 * at + half

            @pl.when(to != z)
            def _():
                remote(
                    partial.at[to], from_z.at[z], z_send.at[to], z_recv.at[z], (me, to)
                ).start()

    total = partial[z].astype(f32)
    for dz in range(1, NZ):
        source = lax.rem(z + dz, NZ)
        copy = remote(
            partial.at[source], from_z.at[source], z_send.at[source], z_recv.at[source], (me, source)
        )
        copy.wait_send()
        copy.wait_recv()
        total = total + from_z[source].astype(f32)
    out_ref[...] = total.astype(jnp.bfloat16)
    for copy in sends:
        copy.wait_send()


def combine(parts, out_weight):
    vmem = pl.BlockSpec(memory_space=pltpu.VMEM)
    bf16 = jnp.bfloat16
    dma = pltpu.SemaphoreType.DMA
    return pl.pallas_call(
        combine_kernel,
        out_shape=jax.ShapeDtypeStruct((SPAN // NZ, HEAD_SIZE), bf16),
        in_specs=[pl.BlockSpec(memory_space=pl.ANY), vmem],
        out_specs=vmem,
        scratch_shapes=[
            pltpu.VMEM((QUERY_BLOCK, WIDE), bf16),
            pltpu.VMEM((NX, QUERY_BLOCK, WIDE), bf16),
            pltpu.VMEM((NY, CHIP_TOKENS, WIDE), bf16),
            pltpu.VMEM((NY, CHIP_TOKENS, WIDE), bf16),
            pltpu.VMEM((NX, 2, NY, CHIP_TOKENS, HALF), bf16),
            pltpu.VMEM((NZ, SPAN // NZ, HEAD_SIZE), bf16),
            pltpu.VMEM((NZ, SPAN // NZ, HEAD_SIZE), bf16),
            dma,
            dma((NX,)),
            dma((NX,)),
            dma((NY,)),
            dma((NY,)),
            dma((NY,)),
            dma((NY,)),
            dma((NX, NY)),
            dma((NX, NY)),
            dma((NX,)),
            dma((NX,)),
            dma((NZ,)),
            dma((NZ,)),
        ],
        compiler_params=pltpu.CompilerParams(collective_id=1, has_side_effects=True),
        name="combine_rows",
    )(parts, out_weight)


def local(
    queries, fresh_span_keys, fresh_span_values, context_keys, context_values, selected, out_weight
):
    q_all, span_keys, span_values, pair_k, pair_v = gather(
        queries, fresh_span_keys, fresh_span_values, context_keys, context_values
    )
    parts = attend(
        selected,
        q_all.reshape(SPAN, HALF),
        span_keys.reshape(CHIP_TOKENS, HEAD_SIZE),
        span_values.reshape(CHIP_TOKENS, HEAD_SIZE),
        context_keys,
        context_values,
        pair_k,
        pair_v,
    )
    return combine(parts, out_weight)


def solution(mesh):
    return jax.shard_map(
        local,
        mesh=mesh,
        in_specs=(
            P("ctx", "head"),
            P("ctx", "head"),
            P("ctx", "head"),
            P("ctx", "head"),
            P("ctx", "head"),
            P(),
            P("head", "ctx"),
        ),
        out_specs=P("head", "ctx"),
        check_vma=False,
    )
```

```python
import math

import jax
import jax.numpy as jnp
from jax import lax
from jax.experimental import pallas as pl
from jax.experimental.pallas import tpu as pltpu
from jax.sharding import PartitionSpec as P

HEAD_SIZE = 128
BLOCK_TOKENS = 4096
QUERY_BLOCK = 128
QUERY_BLOCKS = 4
PICKED = 12
SPAN = 512
NX, NY, NZ = 4, 8, 8
CORE_HEADS = 4
HALF = CORE_HEADS * HEAD_SIZE
WIDE = HALF + HEAD_SIZE
CHIP_TOKENS = 16
HALF_ROWS = QUERY_BLOCK // 2
ROWS = CORE_HEADS * QUERY_BLOCK
KEY_PIECE = 1024
PIECES = BLOCK_TOKENS // KEY_PIECE
TILES = KEY_PIECE // HEAD_SIZE

EXP2_SCALE = math.log2(math.e) / math.sqrt(HEAD_SIZE)
NEG = -(2.0**100)
NEAR_FIRST = (1, 7, 2, 6, 3, 5, 4)
MESH = pl.DeviceIdType.MESH


def place():
    me = lax.axis_index("ctx")
    core = lax.rem(me, 2)
    chip = me // 2
    return me, chip // NY, lax.rem(chip, NY), core, lax.axis_index("head")


def greet(ids):
    barrier = pltpu.get_barrier_semaphore()
    for device in ids:
        pl.semaphore_signal(barrier, inc=1, device_id=device, device_id_type=MESH)
    pl.semaphore_wait(barrier, len(ids))


def remote(src, dst, send, recv, device):
    return pltpu.make_async_remote_copy(
        src_ref=src,
        dst_ref=dst,
        send_sem=send,
        recv_sem=recv,
        device_id=device,
        device_id_type=MESH,
    )


def spread(spot, device, y_send, y_recv, x_send, x_recv):
    sends = []

    def go(at, send, recv, to):
        copy = remote(at, at, send, recv, to)
        copy.start()
        sends.append(copy)

    def arrive(at, send, recv):
        remote(at, at, send, recv, device(0, 1)).wait_recv()

    def forward(n, dy):
        dx = 1 if n % 2 == 0 else 3
        arrive(spot(dx, dy), x_send.at[dx, dy], x_recv.at[dx, dy])
        go(spot(dx, dy), x_send.at[2, dy], x_recv.at[2, dy], device(dx, 0))

    for dy in (4, 3, 5, 2, 6, 1, 7):
        go(spot(0, 0), y_send.at[dy], y_recv.at[dy], device(0, dy))
    order = (0,) + NEAR_FIRST
    for n, dy in enumerate(order):
        if dy:
            arrive(spot(0, dy), y_send.at[dy], y_recv.at[dy])
        for dx in (1, 3):
            go(spot(0, dy), x_send.at[dx, dy], x_recv.at[dx, dy], device(dx, 0))
        if n >= 2:
            forward(n - 2, order[n - 2])
    for n in (6, 7):
        forward(n, order[n])
    for n, dy in enumerate(order):
        dx = 3 if n % 2 == 0 else 1
        arrive(spot(dx, dy), x_send.at[dx, dy], x_recv.at[dx, dy])
        arrive(spot(2, dy), x_send.at[2, dy], x_recv.at[2, dy])
    return sends


def gather_kernel(
    q_ref,
    fk_ref,
    fv_ref,
    ck_ref,
    cv_ref,
    qall_ref,
    sk_ref,
    sv_ref,
    pk_ref,
    pv_ref,
    own_sem,
    pair_send,
    pair_recv,
    y_send,
    y_recv,
    x_send,
    x_recv,
):
    me, x, y, core, z = place()
    chip = me // 2
    other = me + 1 - 2 * core

    def device(dx, dy):
        return ((lax.rem(x + dx, NX) * NY + lax.rem(y + dy, NY)) * 2 + core, z)

    def chunk(dx, dy):
        row = lax.rem(x + NX - dx, NX) * NY + lax.rem(y + NY - dy, NY)
        return qall_ref.at[pl.ds(row * 2, 2)]

    greet(
        [(other, z)]
        + [device(0, dy) for dy in range(1, NY)]
        + [device(dx, 0) for dx in range(1, NX)]
    )

    own_half = q_ref.at[:, pl.ds(pl.multiple_of(core * HALF, HALF), HALF)]
    other_half = q_ref.at[:, pl.ds(pl.multiple_of((1 - core) * HALF, HALF), HALF)]
    pairs = [
        remote(src, dst, pair_send.at[n], pair_recv.at[n], (other, z))
        for n, (src, dst) in enumerate(
            (
                (other_half, qall_ref.at[me]),
                (fk_ref, sk_ref.at[core]),
                (fv_ref, sv_ref.at[core]),
                (ck_ref, pk_ref),
                (cv_ref, pv_ref),
            )
        )
    ]
    owns = [
        pltpu.make_async_copy(src, dst, own_sem.at[n])
        for n, (src, dst) in enumerate(
            (
                (own_half, qall_ref.at[me]),
                (fk_ref, sk_ref.at[core]),
                (fv_ref, sv_ref.at[core]),
            )
        )
    ]
    pairs[0].start()
    for copy in owns:
        copy.start()
    for copy in pairs[1:]:
        copy.start()
    owns[0].wait()
    remote(
        other_half, qall_ref.at[other], pair_send.at[0], pair_recv.at[0], (other, z)
    ).wait_recv()

    sends = spread(chunk, device, y_send, y_recv, x_send, x_recv)
    for copy in sends:
        copy.wait_send()
    for copy in owns[1:]:
        copy.wait()
    pairs[0].wait_send()
    spots = (sk_ref.at[1 - core], sv_ref.at[1 - core], pk_ref, pv_ref)
    for n, copy in enumerate(pairs[1:]):
        copy.wait_send()
        remote(
            spots[n], spots[n], pair_send.at[n + 1], pair_recv.at[n + 1], (other, z)
        ).wait_recv()


def gather(queries, fresh_keys, fresh_values, cache_keys, cache_values):
    anywhere = pl.BlockSpec(memory_space=pl.ANY)
    bf16 = jnp.bfloat16
    dma = pltpu.SemaphoreType.DMA
    return pl.pallas_call(
        gather_kernel,
        out_shape=(
            jax.ShapeDtypeStruct((2 * NX * NY, 8, HALF), bf16),
            jax.ShapeDtypeStruct((2, 8, HEAD_SIZE), bf16),
            jax.ShapeDtypeStruct((2, 8, HEAD_SIZE), bf16),
            jax.ShapeDtypeStruct((BLOCK_TOKENS, HEAD_SIZE), bf16),
            jax.ShapeDtypeStruct((BLOCK_TOKENS, HEAD_SIZE), bf16),
        ),
        in_specs=[anywhere] * 5,
        out_specs=[anywhere] * 5,
        scratch_shapes=[
            dma((3,)),
            dma((5,)),
            dma((5,)),
            dma((NY,)),
            dma((NY,)),
            dma((NX, NY)),
            dma((NX, NY)),
        ],
        compiler_params=pltpu.CompilerParams(collective_id=0, has_side_effects=True),
        name="gather_spans",
    )(queries, fresh_keys, fresh_values, cache_keys, cache_values)


def attend_kernel(
    sel_ref,
    q_ref,
    sk_ref,
    sv_ref,
    ck_ref,
    cv_ref,
    pk_ref,
    pv_ref,
    out_ref,
    kbuf,
    vbuf,
    qs,
    m_s,
    l_s,
    acc_s,
    s_buf,
    top_buf,
    sems,
):
    me, x, y, core, z = place()
    chip = me // 2
    copies = [
        pltpu.make_async_copy(src, dst, sems.at[n])
        for n, (src, dst) in enumerate(
            (
                (ck_ref, kbuf.at[0]),
                (cv_ref, vbuf.at[0, :, pl.ds(0, HEAD_SIZE)]),
                (pk_ref, kbuf.at[1]),
                (pv_ref, vbuf.at[1, :, pl.ds(0, HEAD_SIZE)]),
            )
        )
    ]
    for copy in copies:
        copy.start()

    vbuf[:, :, HEAD_SIZE:] = jnp.ones((2, BLOCK_TOKENS, HEAD_SIZE), jnp.bfloat16)
    stat_lane = lax.broadcasted_iota(jnp.int32, (QUERY_BLOCK, HEAD_SIZE), 1)

    @pl.loop(0, QUERY_BLOCKS)
    def _(j):
        start = pl.multiple_of(j * QUERY_BLOCK, QUERY_BLOCK)
        for g in range(CORE_HEADS):
            qs[g * QUERY_BLOCK : (g + 1) * QUERY_BLOCK] = q_ref[
                pl.ds(start, QUERY_BLOCK), g * HEAD_SIZE : (g + 1) * HEAD_SIZE
            ]
        m_s[...] = jnp.full_like(m_s, NEG)
        l_s[...] = jnp.zeros_like(l_s)
        acc_s[...] = jnp.zeros_like(acc_s)

        @pl.when(j >= x)
        def _():
            s = lax.dot_general(
                qs[...], sk_ref[...], (((1,), (1,)), ((), ())), preferred_element_type=jnp.float32
            )
            token = j * QUERY_BLOCK + lax.rem(
                lax.broadcasted_iota(jnp.int32, s.shape, 0), QUERY_BLOCK
            )
            key = chip * CHIP_TOKENS + lax.broadcasted_iota(jnp.int32, s.shape, 1)
            keep = key <= token
            s = jnp.where(keep, s, NEG)
            m = jnp.max(s, axis=1, keepdims=True)
            p = jnp.where(keep, jnp.exp2((s - m) * EXP2_SCALE), 0.0)
            m_s[...] = jnp.broadcast_to(m, m_s.shape)
            l_s[...] = jnp.broadcast_to(jnp.sum(p, axis=1, keepdims=True), l_s.shape)
            acc_s[...] = jnp.dot(
                p.astype(jnp.bfloat16), sv_ref[...], preferred_element_type=jnp.float32
            )

        @pl.when(j == 0)
        def _():
            for copy in copies:
                copy.wait()

        @pl.loop(0, 2)
        def _(b):
            block = jnp.where(b == 0, me, me + 1 - 2 * core)
            wanted = sel_ref[j, 0] == block
            for n in range(1, PICKED):
                wanted = jnp.logical_or(wanted, sel_ref[j, n] == block)

            def score(n):
                keys = kbuf[b, n * KEY_PIECE : (n + 1) * KEY_PIECE, :]
                scores = lax.dot_general(
                    qs[...], keys, (((1,), (1,)), ((), ())), preferred_element_type=jnp.float32
                )
                s_buf[n % 2] = scores
                top = scores[:, :HEAD_SIZE]
                for t in range(1, TILES):
                    top = jnp.maximum(top, scores[:, t * HEAD_SIZE : (t + 1) * HEAD_SIZE])
                top_buf[n % 2] = top

            def weigh(n):
                m_old = m_s[...]
                m_new = jnp.maximum(m_old, jnp.max(top_buf[n % 2], axis=1, keepdims=True))
                shrink = jnp.exp2((m_old - m_new) * EXP2_SCALE)
                m_s[...] = m_new
                parts = []
                for t in range(TILES):
                    part = jnp.exp2(
                        (s_buf[n % 2, :, t * HEAD_SIZE : (t + 1) * HEAD_SIZE] - m_new) * EXP2_SCALE
                    )
                    parts.append(part.astype(jnp.bfloat16))
                both = jnp.dot(
                    jnp.concatenate(parts, axis=1),
                    vbuf[b, n * KEY_PIECE : (n + 1) * KEY_PIECE, :],
                    preferred_element_type=jnp.float32,
                )
                acc_s[...] = acc_s[...] * shrink + both[:, :HEAD_SIZE]
                l_s[...] = l_s[...] * shrink + both[:, HEAD_SIZE:]

            @pl.when(wanted)
            def _():
                score(0)
                for n in range(PIECES):
                    if n + 1 < PIECES:
                        score(n + 1)
                    weigh(n)

        m = m_s[...]
        m_sent = m.astype(jnp.bfloat16).astype(jnp.float32)
        grow = jnp.exp2((m - m_sent) * EXP2_SCALE)
        total = l_s[...] * grow
        high = total.astype(jnp.bfloat16).astype(jnp.float32)
        low = total - high
        acc = acc_s[...] * grow
        stats = jnp.zeros((QUERY_BLOCK, HEAD_SIZE), jnp.float32)
        for g in range(CORE_HEADS):
            here = slice(g * QUERY_BLOCK, (g + 1) * QUERY_BLOCK)
            out_ref[j, :, g * HEAD_SIZE : (g + 1) * HEAD_SIZE] = acc[here].astype(jnp.bfloat16)
            stats = jnp.where(stat_lane == g, m_sent[here], stats)
            stats = jnp.where(stat_lane == CORE_HEADS + g, high[here], stats)
            stats = jnp.where(stat_lane == 2 * CORE_HEADS + g, low[here], stats)
        out_ref[j, :, HALF:WIDE] = stats.astype(jnp.bfloat16)


def attend(selected, q_all, span_keys, span_values, own_k, own_v, pair_k, pair_v):
    anywhere = pl.BlockSpec(memory_space=pl.ANY)
    vmem = pl.BlockSpec(memory_space=pltpu.VMEM)
    f32 = jnp.float32
    return pl.pallas_call(
        attend_kernel,
        out_shape=jax.ShapeDtypeStruct((QUERY_BLOCKS, QUERY_BLOCK, WIDE), jnp.bfloat16),
        in_specs=[pl.BlockSpec(memory_space=pltpu.SMEM), vmem, vmem, vmem] + [anywhere] * 4,
        out_specs=vmem,
        scratch_shapes=[
            pltpu.VMEM((2, BLOCK_TOKENS, HEAD_SIZE), jnp.bfloat16),
            pltpu.VMEM((2, BLOCK_TOKENS, 2 * HEAD_SIZE), jnp.bfloat16),
            pltpu.VMEM((ROWS, HEAD_SIZE), jnp.bfloat16),
            pltpu.VMEM((ROWS, HEAD_SIZE), f32),
            pltpu.VMEM((ROWS, HEAD_SIZE), f32),
            pltpu.VMEM((ROWS, HEAD_SIZE), f32),
            pltpu.VMEM((2, ROWS, KEY_PIECE), f32),
            pltpu.VMEM((2, ROWS, HEAD_SIZE), f32),
            pltpu.SemaphoreType.DMA((4,)),
        ],
        name="attend_blocks",
    )(selected, q_all, span_keys, span_values, own_k, own_v, pair_k, pair_v)


def merge(pieces):
    stats = [piece[:, HALF:WIDE].astype(jnp.float32) for piece in pieces]
    joined = []
    for g in range(CORE_HEADS):
        tops = [stat[:, g : g + 1] for stat in stats]
        top = tops[0]
        for one in tops[1:]:
            top = jnp.maximum(top, one)
        total = jnp.zeros_like(top)
        acc = None
        for piece, stat, one in zip(pieces, stats, tops):
            weight = jnp.exp2((one - top) * EXP2_SCALE)
            total = total + weight * (
                stat[:, CORE_HEADS + g : CORE_HEADS + g + 1]
                + stat[:, 2 * CORE_HEADS + g : 2 * CORE_HEADS + g + 1]
            )
            term = weight * piece[:, g * HEAD_SIZE : (g + 1) * HEAD_SIZE].astype(jnp.float32)
            acc = term if acc is None else acc + term
        joined.append((top, total, acc))
    return joined


def combine_kernel(
    part_ref,
    w_ref,
    out_ref,
    own,
    from_x,
    relay,
    near,
    passed,
    merged,
    from_y,
    rows,
    partial,
    from_z,
    own_sem,
    x_send,
    x_recv,
    y_send,
    y_recv,
    ay_send,
    ay_recv,
    ax_send,
    ax_recv,
    c_send,
    c_recv,
    z_send,
    z_recv,
):
    me, x, y, core, z = place()
    other = me + 1 - 2 * core
    f32 = jnp.float32

    def device(dx, dy):
        return ((lax.rem(x + dx, NX) * NY + lax.rem(y + dy, NY)) * 2 + core, z)

    greet(
        [(other, z)]
        + [device(0, dy) for dy in range(1, NY)]
        + [device(dx, 0) for dx in range(1, NX)]
        + [(me, lax.rem(z + dz, NZ)) for dz in range(1, NZ)]
    )
    sends = []

    right, left, far = lax.rem(x + 1, NX), lax.rem(x + 3, NX), lax.rem(x + 2, NX)
    low, high_rows = pl.ds(0, HALF_ROWS), pl.ds(HALF_ROWS, HALF_ROWS)

    def send_x(n, src, dst, dx):
        copy = remote(src, dst, x_send.at[n], x_recv.at[n], device(dx, 0))
        copy.start()
        sends.append(copy)

    def arrive_x(n, at):
        remote(at, at, x_send.at[n], x_recv.at[n], device(1, 0)).wait_recv()

    send_x(0, part_ref.at[far, low], relay.at[0], 1)
    send_x(1, part_ref.at[far, high_rows], relay.at[1], 3)
    send_x(2, part_ref.at[right, high_rows], from_x.at[0, high_rows], 1)
    send_x(3, part_ref.at[left, low], from_x.at[1, low], 3)
    mine = [
        pltpu.make_async_copy(src, dst, own_sem.at[n])
        for n, (src, dst) in enumerate(
            (
                (part_ref.at[x], own),
                (part_ref.at[right, low], near.at[0]),
                (part_ref.at[left, high_rows], near.at[1]),
            )
        )
    ]
    for copy in mine:
        copy.start()
    for copy in mine:
        copy.wait()

    def join(dst, pieces, here):
        joined = merge([piece[here, :] for piece in pieces])
        stats = jnp.zeros((CHIP_TOKENS, HEAD_SIZE), f32)
        for g, (top, total, acc) in enumerate(joined):
            high = total.astype(jnp.bfloat16).astype(f32)
            stats = jnp.where(stat_lane == g, top, stats)
            stats = jnp.where(stat_lane == CORE_HEADS + g, high, stats)
            stats = jnp.where(stat_lane == 2 * CORE_HEADS + g, total - high, stats)
            dst[:, g * HEAD_SIZE : (g + 1) * HEAD_SIZE] = acc.astype(jnp.bfloat16)
        dst[:, HALF:WIDE] = stats.astype(jnp.bfloat16)

    stat_lane = lax.broadcasted_iota(jnp.int32, (CHIP_TOKENS, HEAD_SIZE), 1)
    for side, dx in ((0, 1), (1, 3)):
        arrive_x(side, relay.at[side])

        @pl.loop(0, HALF_ROWS // CHIP_TOKENS)
        def _(n):
            here = pl.ds(pl.multiple_of(n * CHIP_TOKENS, CHIP_TOKENS), CHIP_TOKENS)
            join(passed.at[side, here], [near.at[side], relay.at[side]], here)

        rows_at = low if side == 0 else high_rows
        send_x(4 + side, passed.at[side], from_x.at[side, rows_at], dx)
    arrive_x(2, from_x.at[0, high_rows])
    arrive_x(3, from_x.at[1, low])
    arrive_x(4, from_x.at[0, low])
    arrive_x(5, from_x.at[1, high_rows])

    @pl.loop(1, NY + 1)
    def _(dy):
        at = lax.rem(y + dy, NY)
        here = pl.ds(pl.multiple_of(at * CHIP_TOKENS, CHIP_TOKENS), CHIP_TOKENS)
        join(merged.at[at], [own, from_x.at[0], from_x.at[1]], here)

    for dy in (4, 3, 5, 2, 6, 1, 7):
        copy = remote(
            merged.at[lax.rem(y + dy, NY)],
            from_y.at[dy],
            y_send.at[dy],
            y_recv.at[dy],
            device(0, dy),
        )
        copy.start()
        sends.append(copy)
    for dy in range(1, NY):
        remote(
            from_y.at[dy], from_y.at[dy], y_send.at[dy], y_recv.at[dy], device(0, dy)
        ).wait_recv()
    joined = merge([merged[y]] + [from_y[dy] for dy in range(1, NY)])
    for g, (_, total, acc) in enumerate(joined):
        rows[x, core, y, :, g * HEAD_SIZE : (g + 1) * HEAD_SIZE] = (acc / total).astype(
            jnp.bfloat16
        )

    def spot(dx, dy):
        return rows.at[lax.rem(x + NX - dx, NX), core, lax.rem(y + NY - dy, NY)]

    sends += spread(spot, device, ay_send, ay_recv, ax_send, ax_recv)
    for dx in (0, 1, 3, 2):
        at = lax.rem(x + NX - dx, NX)
        copy = remote(
            rows.at[at, core], rows.at[at, core], c_send.at[dx], c_recv.at[dx], (other, z)
        )
        copy.start()
        sends.append(copy)
        remote(
            rows.at[at, 1 - core], rows.at[at, 1 - core], c_send.at[dx], c_recv.at[dx], (other, z)
        ).wait_recv()
        product = jnp.dot(
            rows[at, 0].reshape(QUERY_BLOCK, HALF), w_ref[:HALF, :], preferred_element_type=f32
        ) + jnp.dot(
            rows[at, 1].reshape(QUERY_BLOCK, HALF), w_ref[HALF:, :], preferred_element_type=f32
        )
        product = product.astype(jnp.bfloat16)
        for half in range(2):
            to = 2 * at + half
            partial[to] = product[half * 64 : (half + 1) * 64]
        for half in range(2):
            to = 2 * at + half

            @pl.when(to != z)
            def _():
                remote(
                    partial.at[to], from_z.at[z], z_send.at[to], z_recv.at[z], (me, to)
                ).start()

    total = partial[z].astype(f32)
    for dz in range(1, NZ):
        source = lax.rem(z + dz, NZ)
        copy = remote(
            partial.at[source], from_z.at[source], z_send.at[source], z_recv.at[source], (me, source)
        )
        copy.wait_send()
        copy.wait_recv()
        total = total + from_z[source].astype(f32)
    out_ref[...] = total.astype(jnp.bfloat16)
    for copy in sends:
        copy.wait_send()


def combine(parts, out_weight):
    vmem = pl.BlockSpec(memory_space=pltpu.VMEM)
    bf16 = jnp.bfloat16
    dma = pltpu.SemaphoreType.DMA
    return pl.pallas_call(
        combine_kernel,
        out_shape=jax.ShapeDtypeStruct((SPAN // NZ, HEAD_SIZE), bf16),
        in_specs=[pl.BlockSpec(memory_space=pl.ANY), vmem],
        out_specs=vmem,
        scratch_shapes=[
            pltpu.VMEM((QUERY_BLOCK, WIDE), bf16),
            pltpu.VMEM((2, QUERY_BLOCK, WIDE), bf16),
            pltpu.VMEM((2, HALF_ROWS, WIDE), bf16),
            pltpu.VMEM((2, HALF_ROWS, WIDE), bf16),
            pltpu.VMEM((2, HALF_ROWS, WIDE), bf16),
            pltpu.VMEM((NY, CHIP_TOKENS, WIDE), bf16),
            pltpu.VMEM((NY, CHIP_TOKENS, WIDE), bf16),
            pltpu.VMEM((NX, 2, NY, CHIP_TOKENS, HALF), bf16),
            pltpu.VMEM((NZ, SPAN // NZ, HEAD_SIZE), bf16),
            pltpu.VMEM((NZ, SPAN // NZ, HEAD_SIZE), bf16),
            dma((3,)),
            dma((6,)),
            dma((6,)),
            dma((NY,)),
            dma((NY,)),
            dma((NY,)),
            dma((NY,)),
            dma((NX, NY)),
            dma((NX, NY)),
            dma((NX,)),
            dma((NX,)),
            dma((NZ,)),
            dma((NZ,)),
        ],
        compiler_params=pltpu.CompilerParams(collective_id=1, has_side_effects=True),
        name="combine_rows",
    )(parts, out_weight)


def local(
    queries, fresh_span_keys, fresh_span_values, context_keys, context_values, selected, out_weight
):
    q_all, span_keys, span_values, pair_k, pair_v = gather(
        queries, fresh_span_keys, fresh_span_values, context_keys, context_values
    )
    parts = attend(
        selected,
        q_all.reshape(SPAN, HALF),
        span_keys.reshape(CHIP_TOKENS, HEAD_SIZE),
        span_values.reshape(CHIP_TOKENS, HEAD_SIZE),
        context_keys,
        context_values,
        pair_k,
        pair_v,
    )
    return combine(parts, out_weight)


def solution(mesh):
    return jax.shard_map(
        local,
        mesh=mesh,
        in_specs=(
            P("ctx", "head"),
            P("ctx", "head"),
            P("ctx", "head"),
            P("ctx", "head"),
            P("ctx", "head"),
            P(),
            P("head", "ctx"),
        ),
        out_specs=P("head", "ctx"),
        check_vma=False,
    )
```

```python
import math

import jax
import jax.numpy as jnp
from jax import lax
from jax.experimental import pallas as pl
from jax.experimental.pallas import tpu as pltpu
from jax.sharding import PartitionSpec as P

HEAD_SIZE = 128
BLOCK_TOKENS = 4096
QUERY_BLOCK = 128
QUERY_BLOCKS = 4
PICKED = 12
SPAN = 512
NX, NY, NZ = 4, 8, 8
CORE_HEADS = 4
HALF = CORE_HEADS * HEAD_SIZE
WIDE = HALF + HEAD_SIZE
CHIP_TOKENS = 16
ROWS = CORE_HEADS * QUERY_BLOCK
KEY_PIECE = 1024
PIECES = BLOCK_TOKENS // KEY_PIECE
TILES = KEY_PIECE // HEAD_SIZE

EXP2_SCALE = math.log2(math.e) / math.sqrt(HEAD_SIZE)
NEG = -(2.0**100)
NEAR_FIRST = (1, 7, 2, 6, 3, 5, 4)
MESH = pl.DeviceIdType.MESH


def place():
    me = lax.axis_index("ctx")
    core = lax.rem(me, 2)
    chip = me // 2
    return me, chip // NY, lax.rem(chip, NY), core, lax.axis_index("head")


def greet(ids):
    barrier = pltpu.get_barrier_semaphore()
    for device in ids:
        pl.semaphore_signal(barrier, inc=1, device_id=device, device_id_type=MESH)
    pl.semaphore_wait(barrier, len(ids))


def remote(src, dst, send, recv, device):
    return pltpu.make_async_remote_copy(
        src_ref=src,
        dst_ref=dst,
        send_sem=send,
        recv_sem=recv,
        device_id=device,
        device_id_type=MESH,
    )


def gather_kernel(
    q_ref,
    fk_ref,
    fv_ref,
    ck_ref,
    cv_ref,
    qall_ref,
    sk_ref,
    sv_ref,
    pk_ref,
    pv_ref,
    own_sem,
    pair_send,
    pair_recv,
    y_send,
    y_recv,
    x_send,
    x_recv,
):
    me, x, y, core, z = place()
    chip = me // 2
    other = me + 1 - 2 * core

    def device(dx, dy, to=core):
        return ((lax.rem(x + dx, NX) * NY + lax.rem(y + dy, NY)) * 2 + to, z)

    def share(dx, dy):
        return lax.rem(x + NX - dx, NX) * NY + lax.rem(y + NY - dy, NY)

    def chunk(dx, dy):
        return qall_ref.at[pl.ds(share(dx, dy) * 2, 2)]

    greet(
        [(other, z)]
        + [device(0, dy) for dy in range(1, NY)]
        + [device(0, dy, 1 - core) for dy in range(1, NY)]
        + [device(dx, 0) for dx in range(1, NX)]
    )

    own_half = q_ref.at[:, pl.ds(pl.multiple_of(core * HALF, HALF), HALF)]
    other_half = q_ref.at[:, pl.ds(pl.multiple_of((1 - core) * HALF, HALF), HALF)]
    pairs = [
        remote(src, dst, pair_send.at[n], pair_recv.at[n], (other, z))
        for n, (src, dst) in enumerate(
            (
                (other_half, qall_ref.at[me]),
                (fk_ref, sk_ref.at[core]),
                (fv_ref, sv_ref.at[core]),
                (ck_ref, pk_ref),
                (cv_ref, pv_ref),
            )
        )
    ]
    owns = [
        pltpu.make_async_copy(src, dst, own_sem.at[n])
        for n, (src, dst) in enumerate(
            (
                (own_half, qall_ref.at[me]),
                (fk_ref, sk_ref.at[core]),
                (fv_ref, sv_ref.at[core]),
            )
        )
    ]
    pairs[0].start()
    for copy in owns:
        copy.start()
    sends = []
    for dy in (4, 3, 5, 2, 6, 1, 7):
        for side, (src, to) in enumerate(((own_half, core), (other_half, 1 - core))):
            copy = remote(
                src, qall_ref.at[me], y_send.at[side, dy], y_recv.at[side, dy], device(0, dy, to)
            )
            copy.start()
            sends.append(copy)
    for copy in pairs[1:]:
        copy.start()
    owns[0].wait()
    remote(
        other_half, qall_ref.at[other], pair_send.at[0], pair_recv.at[0], (other, z)
    ).wait_recv()

    def along_x(dx, dy):
        copy = remote(
            chunk(0, dy), chunk(0, dy), x_send.at[dx, dy], x_recv.at[dx, dy], device(dx, 0)
        )
        copy.start()
        sends.append(copy)

    for dx in (2, 1, 3):
        along_x(dx, 0)
    for dy in NEAR_FIRST:
        for side, at in enumerate((core, 1 - core)):
            slab = qall_ref.at[share(0, dy) * 2 + at]
            remote(
                own_half, slab, y_send.at[side, dy], y_recv.at[side, dy], device(0, dy)
            ).wait_recv()
        for dx in (2, 1, 3):
            along_x(dx, dy)
    for dy in (0,) + NEAR_FIRST:
        for dx in (1, 3, 2):
            remote(
                chunk(dx, dy), chunk(dx, dy), x_send.at[dx, dy], x_recv.at[dx, dy], device(dx, 0)
            ).wait_recv()
    for copy in sends:
        copy.wait_send()
    for copy in owns[1:]:
        copy.wait()
    pairs[0].wait_send()
    spots = (sk_ref.at[1 - core], sv_ref.at[1 - core], pk_ref, pv_ref)
    for n, copy in enumerate(pairs[1:]):
        copy.wait_send()
        remote(
            spots[n], spots[n], pair_send.at[n + 1], pair_recv.at[n + 1], (other, z)
        ).wait_recv()


def gather(queries, fresh_keys, fresh_values, cache_keys, cache_values):
    anywhere = pl.BlockSpec(memory_space=pl.ANY)
    bf16 = jnp.bfloat16
    dma = pltpu.SemaphoreType.DMA
    return pl.pallas_call(
        gather_kernel,
        out_shape=(
            jax.ShapeDtypeStruct((2 * NX * NY, 8, HALF), bf16),
            jax.ShapeDtypeStruct((2, 8, HEAD_SIZE), bf16),
            jax.ShapeDtypeStruct((2, 8, HEAD_SIZE), bf16),
            jax.ShapeDtypeStruct((BLOCK_TOKENS, HEAD_SIZE), bf16),
            jax.ShapeDtypeStruct((BLOCK_TOKENS, HEAD_SIZE), bf16),
        ),
        in_specs=[anywhere] * 5,
        out_specs=[anywhere] * 5,
        scratch_shapes=[
            dma((3,)),
            dma((5,)),
            dma((5,)),
            dma((2, NY)),
            dma((2, NY)),
            dma((NX, NY)),
            dma((NX, NY)),
        ],
        compiler_params=pltpu.CompilerParams(collective_id=0, has_side_effects=True),
        name="gather_spans",
    )(queries, fresh_keys, fresh_values, cache_keys, cache_values)


def attend_kernel(
    sel_ref,
    q_ref,
    sk_ref,
    sv_ref,
    ck_ref,
    cv_ref,
    pk_ref,
    pv_ref,
    out_ref,
    kbuf,
    vbuf,
    qs,
    m_s,
    l_s,
    acc_s,
    s_buf,
    top_buf,
    sems,
):
    me, x, y, core, z = place()
    chip = me // 2
    copies = [
        pltpu.make_async_copy(src, dst, sems.at[n])
        for n, (src, dst) in enumerate(
            (
                (ck_ref, kbuf.at[0]),
                (cv_ref, vbuf.at[0, :, pl.ds(0, HEAD_SIZE)]),
                (pk_ref, kbuf.at[1]),
                (pv_ref, vbuf.at[1, :, pl.ds(0, HEAD_SIZE)]),
            )
        )
    ]
    for copy in copies:
        copy.start()

    vbuf[:, :, HEAD_SIZE:] = jnp.ones((2, BLOCK_TOKENS, HEAD_SIZE), jnp.bfloat16)
    stat_lane = lax.broadcasted_iota(jnp.int32, (QUERY_BLOCK, HEAD_SIZE), 1)

    @pl.loop(0, QUERY_BLOCKS)
    def _(j):
        start = pl.multiple_of(j * QUERY_BLOCK, QUERY_BLOCK)
        for g in range(CORE_HEADS):
            qs[g * QUERY_BLOCK : (g + 1) * QUERY_BLOCK] = q_ref[
                pl.ds(start, QUERY_BLOCK), g * HEAD_SIZE : (g + 1) * HEAD_SIZE
            ]
        m_s[...] = jnp.full_like(m_s, NEG)
        l_s[...] = jnp.zeros_like(l_s)
        acc_s[...] = jnp.zeros_like(acc_s)

        @pl.when(j >= x)
        def _():
            s = lax.dot_general(
                qs[...], sk_ref[...], (((1,), (1,)), ((), ())), preferred_element_type=jnp.float32
            )
            token = j * QUERY_BLOCK + lax.rem(
                lax.broadcasted_iota(jnp.int32, s.shape, 0), QUERY_BLOCK
            )
            key = chip * CHIP_TOKENS + lax.broadcasted_iota(jnp.int32, s.shape, 1)
            keep = key <= token
            s = jnp.where(keep, s, NEG)
            m = jnp.max(s, axis=1, keepdims=True)
            p = jnp.where(keep, jnp.exp2((s - m) * EXP2_SCALE), 0.0)
            m_s[...] = jnp.broadcast_to(m, m_s.shape)
            l_s[...] = jnp.broadcast_to(jnp.sum(p, axis=1, keepdims=True), l_s.shape)
            acc_s[...] = jnp.dot(
                p.astype(jnp.bfloat16), sv_ref[...], preferred_element_type=jnp.float32
            )

        @pl.when(j == 0)
        def _():
            for copy in copies:
                copy.wait()

        @pl.loop(0, 2)
        def _(b):
            block = jnp.where(b == 0, me, me + 1 - 2 * core)
            wanted = sel_ref[j, 0] == block
            for n in range(1, PICKED):
                wanted = jnp.logical_or(wanted, sel_ref[j, n] == block)

            def score(n):
                keys = kbuf[b, n * KEY_PIECE : (n + 1) * KEY_PIECE, :]
                scores = lax.dot_general(
                    qs[...], keys, (((1,), (1,)), ((), ())), preferred_element_type=jnp.float32
                )
                s_buf[n % 2] = scores
                top = scores[:, :HEAD_SIZE]
                for t in range(1, TILES):
                    top = jnp.maximum(top, scores[:, t * HEAD_SIZE : (t + 1) * HEAD_SIZE])
                top_buf[n % 2] = top

            def weigh(n):
                m_old = m_s[...]
                m_new = jnp.maximum(m_old, jnp.max(top_buf[n % 2], axis=1, keepdims=True))
                shrink = jnp.exp2((m_old - m_new) * EXP2_SCALE)
                m_s[...] = m_new
                parts = []
                for t in range(TILES):
                    part = jnp.exp2(
                        (s_buf[n % 2, :, t * HEAD_SIZE : (t + 1) * HEAD_SIZE] - m_new) * EXP2_SCALE
                    )
                    parts.append(part.astype(jnp.bfloat16))
                both = jnp.dot(
                    jnp.concatenate(parts, axis=1),
                    vbuf[b, n * KEY_PIECE : (n + 1) * KEY_PIECE, :],
                    preferred_element_type=jnp.float32,
                )
                acc_s[...] = acc_s[...] * shrink + both[:, :HEAD_SIZE]
                l_s[...] = l_s[...] * shrink + both[:, HEAD_SIZE:]

            @pl.when(wanted)
            def _():
                score(0)
                for n in range(PIECES):
                    if n + 1 < PIECES:
                        score(n + 1)
                    weigh(n)

        m = m_s[...]
        m_sent = m.astype(jnp.bfloat16).astype(jnp.float32)
        grow = jnp.exp2((m - m_sent) * EXP2_SCALE)
        total = l_s[...] * grow
        high = total.astype(jnp.bfloat16).astype(jnp.float32)
        low = total - high
        acc = acc_s[...] * grow
        stats = jnp.zeros((QUERY_BLOCK, HEAD_SIZE), jnp.float32)
        for g in range(CORE_HEADS):
            here = slice(g * QUERY_BLOCK, (g + 1) * QUERY_BLOCK)
            out_ref[j, :, g * HEAD_SIZE : (g + 1) * HEAD_SIZE] = acc[here].astype(jnp.bfloat16)
            stats = jnp.where(stat_lane == g, m_sent[here], stats)
            stats = jnp.where(stat_lane == CORE_HEADS + g, high[here], stats)
            stats = jnp.where(stat_lane == 2 * CORE_HEADS + g, low[here], stats)
        out_ref[j, :, HALF:WIDE] = stats.astype(jnp.bfloat16)


def attend(selected, q_all, span_keys, span_values, own_k, own_v, pair_k, pair_v):
    anywhere = pl.BlockSpec(memory_space=pl.ANY)
    vmem = pl.BlockSpec(memory_space=pltpu.VMEM)
    f32 = jnp.float32
    return pl.pallas_call(
        attend_kernel,
        out_shape=jax.ShapeDtypeStruct((QUERY_BLOCKS, QUERY_BLOCK, WIDE), jnp.bfloat16),
        in_specs=[pl.BlockSpec(memory_space=pltpu.SMEM), vmem, vmem, vmem] + [anywhere] * 4,
        out_specs=vmem,
        scratch_shapes=[
            pltpu.VMEM((2, BLOCK_TOKENS, HEAD_SIZE), jnp.bfloat16),
            pltpu.VMEM((2, BLOCK_TOKENS, 2 * HEAD_SIZE), jnp.bfloat16),
            pltpu.VMEM((ROWS, HEAD_SIZE), jnp.bfloat16),
            pltpu.VMEM((ROWS, HEAD_SIZE), f32),
            pltpu.VMEM((ROWS, HEAD_SIZE), f32),
            pltpu.VMEM((ROWS, HEAD_SIZE), f32),
            pltpu.VMEM((2, ROWS, KEY_PIECE), f32),
            pltpu.VMEM((2, ROWS, HEAD_SIZE), f32),
            pltpu.SemaphoreType.DMA((4,)),
        ],
        name="attend_blocks",
    )(selected, q_all, span_keys, span_values, own_k, own_v, pair_k, pair_v)


def merge(pieces):
    stats = [piece[:, HALF:WIDE].astype(jnp.float32) for piece in pieces]
    joined = []
    for g in range(CORE_HEADS):
        tops = [stat[:, g : g + 1] for stat in stats]
        top = tops[0]
        for one in tops[1:]:
            top = jnp.maximum(top, one)
        total = jnp.zeros_like(top)
        acc = None
        for piece, stat, one in zip(pieces, stats, tops):
            weight = jnp.exp2((one - top) * EXP2_SCALE)
            total = total + weight * (
                stat[:, CORE_HEADS + g : CORE_HEADS + g + 1]
                + stat[:, 2 * CORE_HEADS + g : 2 * CORE_HEADS + g + 1]
            )
            term = weight * piece[:, g * HEAD_SIZE : (g + 1) * HEAD_SIZE].astype(jnp.float32)
            acc = term if acc is None else acc + term
        joined.append((top, total, acc))
    return joined


def combine_kernel(
    part_ref,
    w_ref,
    out_ref,
    own,
    from_x,
    merged,
    from_y,
    rows,
    partial,
    from_z,
    own_sem,
    x_send,
    x_recv,
    y_send,
    y_recv,
    ay_send,
    ay_recv,
    ax_send,
    ax_recv,
    c_send,
    c_recv,
    z_send,
    z_recv,
):
    me, x, y, core, z = place()
    other = me + 1 - 2 * core
    f32 = jnp.float32

    def device(dx, dy):
        return ((lax.rem(x + dx, NX) * NY + lax.rem(y + dy, NY)) * 2 + core, z)

    greet(
        [(other, z)]
        + [device(0, dy) for dy in range(1, NY)]
        + [device(dx, 0) for dx in range(1, NX)]
        + [(me, lax.rem(z + dz, NZ)) for dz in range(1, NZ)]
    )
    sends = []

    def turn(n):
        return 4 + (1 - 2 * lax.rem(n, 2)) * ((n + 1) // 2)

    def piece(dy):
        at = lax.rem(y + dy, NY)
        return at, pl.ds(pl.multiple_of(at * CHIP_TOKENS, CHIP_TOKENS), CHIP_TOKENS)

    mine = pltpu.make_async_copy(part_ref.at[x], own, own_sem)
    mine.start()

    def to_x(dx, dy):
        _, here = piece(dy)
        return remote(
            part_ref.at[lax.rem(x + dx, NX), here],
            from_x.at[dx, here],
            x_send.at[dx, dy],
            x_recv.at[dx, dy],
            device(dx, 0),
        )

    def to_y(dy):
        return remote(
            merged.at[lax.rem(y + dy, NY)],
            from_y.at[dy],
            y_send.at[dy],
            y_recv.at[dy],
            device(0, dy),
        )

    @pl.loop(0, NY)
    def _(n):
        for dx in (2, 1, 3):
            to_x(dx, turn(n)).start()

    mine.wait()
    stat_lane = lax.broadcasted_iota(jnp.int32, (CHIP_TOKENS, HEAD_SIZE), 1)

    @pl.loop(0, NY)
    def _(n):
        dy = turn(n)
        at, here = piece(dy)
        for dx in range(1, NX):
            spot = from_x.at[dx, here]
            remote(spot, spot, x_send.at[dx, dy], x_recv.at[dx, dy], device(dx, 0)).wait_recv()
        joined = merge([own[here, :]] + [from_x[dx, here, :] for dx in range(1, NX)])
        stats = jnp.zeros((CHIP_TOKENS, HEAD_SIZE), f32)
        for g, (top, total, acc) in enumerate(joined):
            high = total.astype(jnp.bfloat16).astype(f32)
            stats = jnp.where(stat_lane == g, top, stats)
            stats = jnp.where(stat_lane == CORE_HEADS + g, high, stats)
            stats = jnp.where(stat_lane == 2 * CORE_HEADS + g, total - high, stats)
            merged[at, :, g * HEAD_SIZE : (g + 1) * HEAD_SIZE] = acc.astype(jnp.bfloat16)
        merged[at, :, HALF:WIDE] = stats.astype(jnp.bfloat16)

        @pl.when(n > 0)
        def _():
            to_y(turn(n - 1)).start()

    for dy in range(1, NY):
        remote(
            from_y.at[dy], from_y.at[dy], y_send.at[dy], y_recv.at[dy], device(0, dy)
        ).wait_recv()
    joined = merge([merged[y]] + [from_y[dy] for dy in range(1, NY)])
    for g, (_, total, acc) in enumerate(joined):
        rows[x, core, y, :, g * HEAD_SIZE : (g + 1) * HEAD_SIZE] = (acc / total).astype(
            jnp.bfloat16
        )

    def spot(dx, dy):
        return rows.at[lax.rem(x + NX - dx, NX), core, lax.rem(y + NY - dy, NY)]

    for dy in (4, 3, 5, 2, 6, 1, 7):
        copy = remote(spot(0, 0), spot(0, 0), ay_send.at[dy], ay_recv.at[dy], device(0, dy))
        copy.start()
        sends.append(copy)
    for dy in (0,) + NEAR_FIRST:
        if dy:
            remote(
                spot(0, dy), spot(0, dy), ay_send.at[dy], ay_recv.at[dy], device(0, dy)
            ).wait_recv()
        for dx in (2, 1, 3):
            copy = remote(
                spot(0, dy), spot(0, dy), ax_send.at[dx, dy], ax_recv.at[dx, dy], device(dx, 0)
            )
            copy.start()
            sends.append(copy)
    for dx in (0, 1, 3, 2):
        if dx:
            for dy in (0,) + NEAR_FIRST:
                remote(
                    spot(dx, dy), spot(dx, dy), ax_send.at[dx, dy], ax_recv.at[dx, dy], device(dx, 0)
                ).wait_recv()
        group = rows.at[lax.rem(x + NX - dx, NX), core]
        copy = remote(group, group, c_send.at[dx], c_recv.at[dx], (other, z))
        copy.start()
        sends.append(copy)
    for dx in (0, 1, 3, 2):
        at = lax.rem(x + NX - dx, NX)
        group = rows.at[at, 1 - core]
        remote(group, group, c_send.at[dx], c_recv.at[dx], (other, z)).wait_recv()
        product = jnp.dot(
            rows[at, 0].reshape(QUERY_BLOCK, HALF), w_ref[:HALF, :], preferred_element_type=f32
        ) + jnp.dot(
            rows[at, 1].reshape(QUERY_BLOCK, HALF), w_ref[HALF:, :], preferred_element_type=f32
        )
        product = product.astype(jnp.bfloat16)
        for half in range(2):
            to = 2 * at + half
            partial[to] = product[half * 64 : (half + 1) * 64]
        for half in range(2):
            to = 2 * at + half

            @pl.when(to != z)
            def _():
                remote(
                    partial.at[to], from_z.at[z], z_send.at[to], z_recv.at[z], (me, to)
                ).start()

    total = partial[z].astype(f32)
    for dz in range(1, NZ):
        source = lax.rem(z + dz, NZ)
        copy = remote(
            partial.at[source], from_z.at[source], z_send.at[source], z_recv.at[source], (me, source)
        )
        copy.wait_send()
        copy.wait_recv()
        total = total + from_z[source].astype(f32)
    out_ref[...] = total.astype(jnp.bfloat16)

    @pl.loop(0, NY)
    def _(dy):
        for dx in range(1, NX):
            to_x(dx, dy).wait_send()

        @pl.when(dy > 0)
        def _():
            to_y(dy).wait_send()

    for copy in sends:
        copy.wait_send()


def combine(parts, out_weight):
    vmem = pl.BlockSpec(memory_space=pltpu.VMEM)
    bf16 = jnp.bfloat16
    dma = pltpu.SemaphoreType.DMA
    return pl.pallas_call(
        combine_kernel,
        out_shape=jax.ShapeDtypeStruct((SPAN // NZ, HEAD_SIZE), bf16),
        in_specs=[pl.BlockSpec(memory_space=pl.ANY), vmem],
        out_specs=vmem,
        scratch_shapes=[
            pltpu.VMEM((QUERY_BLOCK, WIDE), bf16),
            pltpu.VMEM((NX, QUERY_BLOCK, WIDE), bf16),
            pltpu.VMEM((NY, CHIP_TOKENS, WIDE), bf16),
            pltpu.VMEM((NY, CHIP_TOKENS, WIDE), bf16),
            pltpu.VMEM((NX, 2, NY, CHIP_TOKENS, HALF), bf16),
            pltpu.VMEM((NZ, SPAN // NZ, HEAD_SIZE), bf16),
            pltpu.VMEM((NZ, SPAN // NZ, HEAD_SIZE), bf16),
            dma,
            dma((NX, NY)),
            dma((NX, NY)),
            dma((NY,)),
            dma((NY,)),
            dma((NY,)),
            dma((NY,)),
            dma((NX, NY)),
            dma((NX, NY)),
            dma((NX,)),
            dma((NX,)),
            dma((NZ,)),
            dma((NZ,)),
        ],
        compiler_params=pltpu.CompilerParams(collective_id=1, has_side_effects=True),
        name="combine_rows",
    )(parts, out_weight)


def local(
    queries, fresh_span_keys, fresh_span_values, context_keys, context_values, selected, out_weight
):
    q_all, span_keys, span_values, pair_k, pair_v = gather(
        queries, fresh_span_keys, fresh_span_values, context_keys, context_values
    )
    parts = attend(
        selected,
        q_all.reshape(SPAN, HALF),
        span_keys.reshape(CHIP_TOKENS, HEAD_SIZE),
        span_values.reshape(CHIP_TOKENS, HEAD_SIZE),
        context_keys,
        context_values,
        pair_k,
        pair_v,
    )
    return combine(parts, out_weight)


def solution(mesh):
    return jax.shard_map(
        local,
        mesh=mesh,
        in_specs=(
            P("ctx", "head"),
            P("ctx", "head"),
            P("ctx", "head"),
            P("ctx", "head"),
            P("ctx", "head"),
            P(),
            P("head", "ctx"),
        ),
        out_specs=P("head", "ctx"),
        check_vma=False,
    )
```

```python
import math

import jax
import jax.numpy as jnp
from jax import lax
from jax.experimental import pallas as pl
from jax.experimental.pallas import tpu as pltpu
from jax.sharding import PartitionSpec as P

HEAD_SIZE = 128
BLOCK_TOKENS = 4096
QUERY_BLOCK = 128
QUERY_BLOCKS = 4
PICKED = 12
SPAN = 512
NX, NY, NZ = 4, 8, 8
CORE_HEADS = 4
HALF = CORE_HEADS * HEAD_SIZE
WIDE = HALF + HEAD_SIZE
CHIP_TOKENS = 16
ROWS = CORE_HEADS * QUERY_BLOCK
KEY_PIECE = 1024
PIECES = BLOCK_TOKENS // KEY_PIECE
TILES = KEY_PIECE // HEAD_SIZE

EXP2_SCALE = math.log2(math.e) / math.sqrt(HEAD_SIZE)
NEG = -(2.0**100)
NEAR_FIRST = (1, 7, 2, 6, 3, 5, 4)
MESH = pl.DeviceIdType.MESH


def place():
    me = lax.axis_index("ctx")
    core = lax.rem(me, 2)
    chip = me // 2
    return me, chip // NY, lax.rem(chip, NY), core, lax.axis_index("head")


def greet(ids):
    barrier = pltpu.get_barrier_semaphore()
    for device in ids:
        pl.semaphore_signal(barrier, inc=1, device_id=device, device_id_type=MESH)
    pl.semaphore_wait(barrier, len(ids))


def remote(src, dst, send, recv, device):
    return pltpu.make_async_remote_copy(
        src_ref=src,
        dst_ref=dst,
        send_sem=send,
        recv_sem=recv,
        device_id=device,
        device_id_type=MESH,
    )


def stack_heads(qs, q_ref, start):
    for g in range(CORE_HEADS):
        qs[g * QUERY_BLOCK : (g + 1) * QUERY_BLOCK] = q_ref[
            pl.ds(start, QUERY_BLOCK), g * HEAD_SIZE : (g + 1) * HEAD_SIZE
        ]


def attend_span(chip, j, state, sk_ref, sv_ref):
    qs, m_s, l_s, acc_s = state
    s = lax.dot_general(
        qs[...], sk_ref[...], (((1,), (1,)), ((), ())), preferred_element_type=jnp.float32
    )
    token = j * QUERY_BLOCK + lax.rem(lax.broadcasted_iota(jnp.int32, s.shape, 0), QUERY_BLOCK)
    key = chip * CHIP_TOKENS + lax.broadcasted_iota(jnp.int32, s.shape, 1)
    keep = key <= token
    s = jnp.where(keep, s, NEG)
    m = jnp.max(s, axis=1, keepdims=True)
    p = jnp.where(keep, jnp.exp2((s - m) * EXP2_SCALE), 0.0)
    m_s[...] = jnp.broadcast_to(m, m_s.shape)
    l_s[...] = jnp.broadcast_to(jnp.sum(p, axis=1, keepdims=True), l_s.shape)
    acc_s[...] = jnp.dot(p.astype(jnp.bfloat16), sv_ref[...], preferred_element_type=jnp.float32)


def attend_block(b, state, kbuf, vbuf, s_buf, top_buf, hide=None):
    qs, m_s, l_s, acc_s = state

    def score(n):
        keys = kbuf[b, n * KEY_PIECE : (n + 1) * KEY_PIECE, :]
        scores = lax.dot_general(
            qs[...], keys, (((1,), (1,)), ((), ())), preferred_element_type=jnp.float32
        )
        s_buf[n % 2] = scores
        top = scores[:, :HEAD_SIZE]
        for t in range(1, TILES):
            top = jnp.maximum(top, scores[:, t * HEAD_SIZE : (t + 1) * HEAD_SIZE])
        top_buf[n % 2] = top

    def weigh(n):
        m_old = m_s[...]
        top = jnp.max(top_buf[n % 2], axis=1, keepdims=True)
        if hide is not None:
            top = top - hide
        m_new = jnp.maximum(m_old, top)
        shrink = jnp.exp2((m_old - m_new) * EXP2_SCALE)
        m_s[...] = m_new
        shift = m_new if hide is None else m_new + hide
        parts = []
        for t in range(TILES):
            part = jnp.exp2(
                (s_buf[n % 2, :, t * HEAD_SIZE : (t + 1) * HEAD_SIZE] - shift) * EXP2_SCALE
            )
            parts.append(part.astype(jnp.bfloat16))
        both = jnp.dot(
            jnp.concatenate(parts, axis=1),
            vbuf[b, n * KEY_PIECE : (n + 1) * KEY_PIECE, :],
            preferred_element_type=jnp.float32,
        )
        acc_s[...] = acc_s[...] * shrink + both[:, :HEAD_SIZE]
        l_s[...] = l_s[...] * shrink + both[:, HEAD_SIZE:]

    score(0)
    for n in range(PIECES):
        if n + 1 < PIECES:
            score(n + 1)
        weigh(n)


def store_partial(out_ref, state):
    _, m_s, l_s, acc_s = state
    stat_lane = lax.broadcasted_iota(jnp.int32, (QUERY_BLOCK, HEAD_SIZE), 1)
    m = m_s[...]
    m_sent = m.astype(jnp.bfloat16).astype(jnp.float32)
    grow = jnp.exp2((m - m_sent) * EXP2_SCALE)
    total = l_s[...] * grow
    high = total.astype(jnp.bfloat16).astype(jnp.float32)
    low = total - high
    acc = acc_s[...] * grow
    stats = jnp.zeros((QUERY_BLOCK, HEAD_SIZE), jnp.float32)
    for g in range(CORE_HEADS):
        here = slice(g * QUERY_BLOCK, (g + 1) * QUERY_BLOCK)
        out_ref[:, g * HEAD_SIZE : (g + 1) * HEAD_SIZE] = acc[here].astype(jnp.bfloat16)
        stats = jnp.where(stat_lane == g, m_sent[here], stats)
        stats = jnp.where(stat_lane == CORE_HEADS + g, high[here], stats)
        stats = jnp.where(stat_lane == 2 * CORE_HEADS + g, low[here], stats)
    out_ref[:, HALF:WIDE] = stats.astype(jnp.bfloat16)


def is_wanted(sel_ref, j, block):
    wanted = sel_ref[j, 0] == block
    for n in range(1, PICKED):
        wanted = jnp.logical_or(wanted, sel_ref[j, n] == block)
    return wanted


def attention_scratch():
    f32 = jnp.float32
    return [
        pltpu.VMEM((2, BLOCK_TOKENS, HEAD_SIZE), jnp.bfloat16),
        pltpu.VMEM((2, BLOCK_TOKENS, 2 * HEAD_SIZE), jnp.bfloat16),
        pltpu.VMEM((ROWS, HEAD_SIZE), jnp.bfloat16),
        pltpu.VMEM((ROWS, HEAD_SIZE), f32),
        pltpu.VMEM((ROWS, HEAD_SIZE), f32),
        pltpu.VMEM((ROWS, HEAD_SIZE), f32),
        pltpu.VMEM((2, ROWS, KEY_PIECE), f32),
        pltpu.VMEM((2, ROWS, HEAD_SIZE), f32),
    ]


def gather_kernel(
    sel_ref,
    q_ref,
    fk_ref,
    fv_ref,
    ck_ref,
    cv_ref,
    qall_ref,
    sk_ref,
    sv_ref,
    pk_ref,
    pv_ref,
    part_ref,
    kbuf,
    vbuf,
    qs,
    m_s,
    l_s,
    acc_s,
    s_buf,
    top_buf,
    q_own,
    sk_own,
    sv_own,
    part_own,
    load_sem,
    own_sem,
    pair_send,
    pair_recv,
    y_send,
    y_recv,
    x_send,
    x_recv,
):
    me, x, y, core, z = place()
    chip = me // 2
    other = me + 1 - 2 * core

    def device(dx, dy, to=core):
        return ((lax.rem(x + dx, NX) * NY + lax.rem(y + dy, NY)) * 2 + to, z)

    def own_span(ref, at):
        return ref.at[pl.ds(pl.multiple_of(at * 8, 8), 8)]

    def share(dx, dy):
        return lax.rem(x + NX - dx, NX) * NY + lax.rem(y + NY - dy, NY)

    def chunk(dx, dy):
        at = pl.multiple_of(share(dx, dy) * CHIP_TOKENS, CHIP_TOKENS)
        return qall_ref.at[pl.ds(at, CHIP_TOKENS)]

    def slab(device_at):
        return qall_ref.at[pl.ds(pl.multiple_of(device_at * 8, 8), 8)]

    greet(
        [(other, z)]
        + [device(0, dy) for dy in range(1, NY)]
        + [device(0, dy, 1 - core) for dy in range(1, NY)]
        + [device(dx, 0) for dx in range(1, NX)]
    )

    own_half = q_ref.at[:, pl.ds(pl.multiple_of(core * HALF, HALF), HALF)]
    other_half = q_ref.at[:, pl.ds(pl.multiple_of((1 - core) * HALF, HALF), HALF)]
    pairs = [
        remote(src, dst, pair_send.at[n], pair_recv.at[n], (other, z))
        for n, (src, dst) in enumerate(
            (
                (other_half, slab(me)),
                (fk_ref, own_span(sk_ref, core)),
                (fv_ref, own_span(sv_ref, core)),
                (ck_ref, pk_ref),
                (cv_ref, pv_ref),
            )
        )
    ]
    owns = [
        pltpu.make_async_copy(src, dst, own_sem.at[n])
        for n, (src, dst) in enumerate(
            (
                (own_half, slab(me)),
                (fk_ref, own_span(sk_ref, core)),
                (fv_ref, own_span(sv_ref, core)),
            )
        )
    ]
    pairs[0].start()
    for copy in owns:
        copy.start()
    sends = []
    for dy in (4, 3, 5, 2, 6, 1, 7):
        for side, (src, to) in enumerate(((own_half, core), (other_half, 1 - core))):
            copy = remote(
                src, slab(me), y_send.at[side, dy], y_recv.at[side, dy], device(0, dy, to)
            )
            copy.start()
            sends.append(copy)
    for copy in pairs[1:]:
        copy.start()

    def load(n, src, dst):
        return pltpu.make_async_copy(src, dst, load_sem.at[n])

    values = pl.ds(0, HEAD_SIZE)
    loads = [
        load(0, ck_ref, kbuf.at[0]),
        load(1, cv_ref, vbuf.at[0, :, values]),
        load(2, pk_ref, kbuf.at[1]),
        load(3, pv_ref, vbuf.at[1, :, values]),
        load(4, qall_ref.at[pl.ds(pl.multiple_of(x * QUERY_BLOCK, QUERY_BLOCK), QUERY_BLOCK)], q_own),
        load(5, sk_ref, sk_own),
        load(6, sv_ref, sv_own),
    ]
    loads[0].start()
    loads[1].start()
    vbuf[:, :, HEAD_SIZE:] = jnp.ones((2, BLOCK_TOKENS, HEAD_SIZE), jnp.bfloat16)
    owns[0].wait()
    remote(
        other_half, slab(other), pair_send.at[0], pair_recv.at[0], (other, z)
    ).wait_recv()

    def along_x(dx, dy):
        copy = remote(
            chunk(0, dy), chunk(0, dy), x_send.at[dx, dy], x_recv.at[dx, dy], device(dx, 0)
        )
        copy.start()
        sends.append(copy)

    for dx in (2, 1, 3):
        along_x(dx, 0)
    for dy in NEAR_FIRST:
        for side, at in enumerate((core, 1 - core)):
            spot = slab(share(0, dy) * 2 + at)
            remote(
                own_half, spot, y_send.at[side, dy], y_recv.at[side, dy], device(0, dy)
            ).wait_recv()
        for dx in (2, 1, 3):
            along_x(dx, dy)
    loads[4].start()
    spots = (own_span(sk_ref, 1 - core), own_span(sv_ref, 1 - core), pk_ref, pv_ref)
    for n, spot in enumerate(spots):
        remote(spot, spot, pair_send.at[n + 1], pair_recv.at[n + 1], (other, z)).wait_recv()
    for copy in owns[1:]:
        copy.wait()
    for n in (5, 6, 2, 3):
        loads[n].start()
    for n in (4, 5, 6):
        loads[n].wait()

    state = (qs, m_s, l_s, acc_s)
    stack_heads(qs, q_own, 0)
    attend_span(chip, x, state, sk_own, sv_own)
    for n in range(4):
        loads[n].wait()

    @pl.loop(0, 2)
    def _(b):
        block = jnp.where(b == 0, me, other)
        hide = jnp.where(is_wanted(sel_ref, x, block), 0.0, -2.0 * NEG)
        attend_block(b, state, kbuf, vbuf, s_buf, top_buf, hide)

    store_partial(part_own, state)
    result = load(7, part_own, part_ref)
    result.start()

    for dy in (0,) + NEAR_FIRST:
        for dx in (1, 3, 2):
            remote(
                chunk(dx, dy), chunk(dx, dy), x_send.at[dx, dy], x_recv.at[dx, dy], device(dx, 0)
            ).wait_recv()
    for copy in sends + pairs:
        copy.wait_send()
    result.wait()


def gather(selected, queries, fresh_keys, fresh_values, cache_keys, cache_values):
    anywhere = pl.BlockSpec(memory_space=pl.ANY)
    bf16 = jnp.bfloat16
    dma = pltpu.SemaphoreType.DMA
    return pl.pallas_call(
        gather_kernel,
        out_shape=(
            jax.ShapeDtypeStruct((SPAN, HALF), bf16),
            jax.ShapeDtypeStruct((CHIP_TOKENS, HEAD_SIZE), bf16),
            jax.ShapeDtypeStruct((CHIP_TOKENS, HEAD_SIZE), bf16),
            jax.ShapeDtypeStruct((BLOCK_TOKENS, HEAD_SIZE), bf16),
            jax.ShapeDtypeStruct((BLOCK_TOKENS, HEAD_SIZE), bf16),
            jax.ShapeDtypeStruct((QUERY_BLOCK, WIDE), bf16),
        ),
        in_specs=[pl.BlockSpec(memory_space=pltpu.SMEM)] + [anywhere] * 5,
        out_specs=[anywhere] * 6,
        scratch_shapes=attention_scratch()
        + [
            pltpu.VMEM((QUERY_BLOCK, HALF), bf16),
            pltpu.VMEM((CHIP_TOKENS, HEAD_SIZE), bf16),
            pltpu.VMEM((CHIP_TOKENS, HEAD_SIZE), bf16),
            pltpu.VMEM((QUERY_BLOCK, WIDE), bf16),
            dma((8,)),
            dma((3,)),
            dma((5,)),
            dma((5,)),
            dma((2, NY)),
            dma((2, NY)),
            dma((NX, NY)),
            dma((NX, NY)),
        ],
        compiler_params=pltpu.CompilerParams(collective_id=0, has_side_effects=True),
        name="gather_spans",
    )(selected, queries, fresh_keys, fresh_values, cache_keys, cache_values)


def attend_kernel(
    sel_ref,
    q_ref,
    sk_ref,
    sv_ref,
    ck_ref,
    cv_ref,
    pk_ref,
    pv_ref,
    out_ref,
    kbuf,
    vbuf,
    qs,
    m_s,
    l_s,
    acc_s,
    s_buf,
    top_buf,
    sems,
):
    me, x, y, core, z = place()
    chip = me // 2
    state = (qs, m_s, l_s, acc_s)
    copies = [
        pltpu.make_async_copy(src, dst, sems.at[n])
        for n, (src, dst) in enumerate(
            (
                (ck_ref, kbuf.at[0]),
                (cv_ref, vbuf.at[0, :, pl.ds(0, HEAD_SIZE)]),
                (pk_ref, kbuf.at[1]),
                (pv_ref, vbuf.at[1, :, pl.ds(0, HEAD_SIZE)]),
            )
        )
    ]
    for copy in copies:
        copy.start()
    vbuf[:, :, HEAD_SIZE:] = jnp.ones((2, BLOCK_TOKENS, HEAD_SIZE), jnp.bfloat16)

    @pl.loop(1, QUERY_BLOCKS)
    def _(n):
        j = lax.rem(x + n, QUERY_BLOCKS)
        stack_heads(qs, q_ref, pl.multiple_of(j * QUERY_BLOCK, QUERY_BLOCK))
        m_s[...] = jnp.full_like(m_s, NEG)
        l_s[...] = jnp.zeros_like(l_s)
        acc_s[...] = jnp.zeros_like(acc_s)

        @pl.when(j > x)
        def _():
            attend_span(chip, j, state, sk_ref, sv_ref)

        @pl.when(n == 1)
        def _():
            for copy in copies:
                copy.wait()

        @pl.loop(0, 2)
        def _(b):
            block = jnp.where(b == 0, me, me + 1 - 2 * core)

            @pl.when(is_wanted(sel_ref, j, block))
            def _():
                attend_block(b, state, kbuf, vbuf, s_buf, top_buf)

        store_partial(out_ref.at[j], state)


def attend(selected, q_all, span_keys, span_values, own_k, own_v, pair_k, pair_v):
    anywhere = pl.BlockSpec(memory_space=pl.ANY)
    vmem = pl.BlockSpec(memory_space=pltpu.VMEM)
    return pl.pallas_call(
        attend_kernel,
        out_shape=jax.ShapeDtypeStruct((QUERY_BLOCKS, QUERY_BLOCK, WIDE), jnp.bfloat16),
        in_specs=[pl.BlockSpec(memory_space=pltpu.SMEM), vmem, vmem, vmem] + [anywhere] * 4,
        out_specs=vmem,
        scratch_shapes=attention_scratch() + [pltpu.SemaphoreType.DMA((4,))],
        name="attend_blocks",
    )(selected, q_all, span_keys, span_values, own_k, own_v, pair_k, pair_v)


def merge(pieces):
    stats = [piece[:, HALF:WIDE].astype(jnp.float32) for piece in pieces]
    joined = []
    for g in range(CORE_HEADS):
        tops = [stat[:, g : g + 1] for stat in stats]
        top = tops[0]
        for one in tops[1:]:
            top = jnp.maximum(top, one)
        total = jnp.zeros_like(top)
        acc = None
        for piece, stat, one in zip(pieces, stats, tops):
            weight = jnp.exp2((one - top) * EXP2_SCALE)
            total = total + weight * (
                stat[:, CORE_HEADS + g : CORE_HEADS + g + 1]
                + stat[:, 2 * CORE_HEADS + g : 2 * CORE_HEADS + g + 1]
            )
            term = weight * piece[:, g * HEAD_SIZE : (g + 1) * HEAD_SIZE].astype(jnp.float32)
            acc = term if acc is None else acc + term
        joined.append((top, total, acc))
    return joined


def combine_kernel(
    own_part_ref,
    part_ref,
    w_ref,
    out_ref,
    own,
    from_x,
    merged,
    from_y,
    rows,
    partial,
    from_z,
    own_sem,
    x_send,
    x_recv,
    y_send,
    y_recv,
    ay_send,
    ay_recv,
    ax_send,
    ax_recv,
    c_send,
    c_recv,
    z_send,
    z_recv,
):
    me, x, y, core, z = place()
    other = me + 1 - 2 * core
    f32 = jnp.float32

    def device(dx, dy):
        return ((lax.rem(x + dx, NX) * NY + lax.rem(y + dy, NY)) * 2 + core, z)

    greet(
        [(other, z)]
        + [device(0, dy) for dy in range(1, NY)]
        + [device(dx, 0) for dx in range(1, NX)]
        + [(me, lax.rem(z + dz, NZ)) for dz in range(1, NZ)]
    )
    sends = []

    def turn(n):
        return 4 + (1 - 2 * lax.rem(n, 2)) * ((n + 1) // 2)

    def piece(dy):
        at = lax.rem(y + dy, NY)
        return at, pl.ds(pl.multiple_of(at * CHIP_TOKENS, CHIP_TOKENS), CHIP_TOKENS)

    mine = pltpu.make_async_copy(own_part_ref, own, own_sem)
    mine.start()

    def to_x(dx, dy):
        _, here = piece(dy)
        return remote(
            part_ref.at[lax.rem(x + dx, NX), here],
            from_x.at[dx, here],
            x_send.at[dx, dy],
            x_recv.at[dx, dy],
            device(dx, 0),
        )

    def to_y(dy):
        return remote(
            merged.at[lax.rem(y + dy, NY)],
            from_y.at[dy],
            y_send.at[dy],
            y_recv.at[dy],
            device(0, dy),
        )

    @pl.loop(0, NY)
    def _(n):
        for dx in (2, 1, 3):
            to_x(dx, turn(n)).start()

    mine.wait()
    stat_lane = lax.broadcasted_iota(jnp.int32, (CHIP_TOKENS, HEAD_SIZE), 1)

    @pl.loop(0, NY)
    def _(n):
        dy = turn(n)
        at, here = piece(dy)
        for dx in range(1, NX):
            spot = from_x.at[dx, here]
            remote(spot, spot, x_send.at[dx, dy], x_recv.at[dx, dy], device(dx, 0)).wait_recv()
        joined = merge([own[here, :]] + [from_x[dx, here, :] for dx in range(1, NX)])
        stats = jnp.zeros((CHIP_TOKENS, HEAD_SIZE), f32)
        for g, (top, total, acc) in enumerate(joined):
            high = total.astype(jnp.bfloat16).astype(f32)
            stats = jnp.where(stat_lane == g, top, stats)
            stats = jnp.where(stat_lane == CORE_HEADS + g, high, stats)
            stats = jnp.where(stat_lane == 2 * CORE_HEADS + g, total - high, stats)
            merged[at, :, g * HEAD_SIZE : (g + 1) * HEAD_SIZE] = acc.astype(jnp.bfloat16)
        merged[at, :, HALF:WIDE] = stats.astype(jnp.bfloat16)

        @pl.when(n > 0)
        def _():
            to_y(turn(n - 1)).start()

    for dy in range(1, NY):
        remote(
            from_y.at[dy], from_y.at[dy], y_send.at[dy], y_recv.at[dy], device(0, dy)
        ).wait_recv()
    joined = merge([merged[y]] + [from_y[dy] for dy in range(1, NY)])
    for g, (_, total, acc) in enumerate(joined):
        rows[x, core, y, :, g * HEAD_SIZE : (g + 1) * HEAD_SIZE] = (acc / total).astype(
            jnp.bfloat16
        )

    def spot(dx, dy):
        return rows.at[lax.rem(x + NX - dx, NX), core, lax.rem(y + NY - dy, NY)]

    for dy in (4, 3, 5, 2, 6, 1, 7):
        copy = remote(spot(0, 0), spot(0, 0), ay_send.at[dy], ay_recv.at[dy], device(0, dy))
        copy.start()
        sends.append(copy)
    for dy in (0,) + NEAR_FIRST:
        if dy:
            remote(
                spot(0, dy), spot(0, dy), ay_send.at[dy], ay_recv.at[dy], device(0, dy)
            ).wait_recv()
        for dx in (2, 1, 3):
            copy = remote(
                spot(0, dy), spot(0, dy), ax_send.at[dx, dy], ax_recv.at[dx, dy], device(dx, 0)
            )
            copy.start()
            sends.append(copy)
    def swap(dx):
        group = rows.at[lax.rem(x + NX - dx, NX), core]
        copy = remote(group, group, c_send.at[dx], c_recv.at[dx], (other, z))
        copy.start()
        sends.append(copy)

    def project(dx):
        at = lax.rem(x + NX - dx, NX)
        group = rows.at[at, 1 - core]
        remote(group, group, c_send.at[dx], c_recv.at[dx], (other, z)).wait_recv()
        product = jnp.dot(
            rows[at, 0].reshape(QUERY_BLOCK, HALF), w_ref[:HALF, :], preferred_element_type=f32
        ) + jnp.dot(
            rows[at, 1].reshape(QUERY_BLOCK, HALF), w_ref[HALF:, :], preferred_element_type=f32
        )
        product = product.astype(jnp.bfloat16)
        for half in range(2):
            partial[2 * at + half] = product[half * 64 : (half + 1) * 64]
        for half in range(2):
            to = 2 * at + half

            @pl.when(to != z)
            def _():
                remote(
                    partial.at[to], from_z.at[z], z_send.at[to], z_recv.at[z], (me, to)
                ).start()

    swap(0)
    project(0)
    for dx in (1, 3, 2):
        for dy in (0,) + NEAR_FIRST:
            remote(
                spot(dx, dy), spot(dx, dy), ax_send.at[dx, dy], ax_recv.at[dx, dy], device(dx, 0)
            ).wait_recv()
        swap(dx)
    for dx in (1, 3, 2):
        project(dx)

    total = partial[z].astype(f32)
    for dz in range(1, NZ):
        source = lax.rem(z + dz, NZ)
        copy = remote(
            partial.at[source], from_z.at[source], z_send.at[source], z_recv.at[source], (me, source)
        )
        copy.wait_send()
        copy.wait_recv()
        total = total + from_z[source].astype(f32)
    out_ref[...] = total.astype(jnp.bfloat16)

    @pl.loop(0, NY)
    def _(dy):
        for dx in range(1, NX):
            to_x(dx, dy).wait_send()

        @pl.when(dy > 0)
        def _():
            to_y(dy).wait_send()

    for copy in sends:
        copy.wait_send()


def combine(own_part, parts, out_weight):
    vmem = pl.BlockSpec(memory_space=pltpu.VMEM)
    bf16 = jnp.bfloat16
    dma = pltpu.SemaphoreType.DMA
    return pl.pallas_call(
        combine_kernel,
        out_shape=jax.ShapeDtypeStruct((SPAN // NZ, HEAD_SIZE), bf16),
        in_specs=[pl.BlockSpec(memory_space=pl.ANY)] * 2 + [vmem],
        out_specs=vmem,
        scratch_shapes=[
            pltpu.VMEM((QUERY_BLOCK, WIDE), bf16),
            pltpu.VMEM((NX, QUERY_BLOCK, WIDE), bf16),
            pltpu.VMEM((NY, CHIP_TOKENS, WIDE), bf16),
            pltpu.VMEM((NY, CHIP_TOKENS, WIDE), bf16),
            pltpu.VMEM((NX, 2, NY, CHIP_TOKENS, HALF), bf16),
            pltpu.VMEM((NZ, SPAN // NZ, HEAD_SIZE), bf16),
            pltpu.VMEM((NZ, SPAN // NZ, HEAD_SIZE), bf16),
            dma,
            dma((NX, NY)),
            dma((NX, NY)),
            dma((NY,)),
            dma((NY,)),
            dma((NY,)),
            dma((NY,)),
            dma((NX, NY)),
            dma((NX, NY)),
            dma((NX,)),
            dma((NX,)),
            dma((NZ,)),
            dma((NZ,)),
        ],
        compiler_params=pltpu.CompilerParams(collective_id=1, has_side_effects=True),
        name="combine_rows",
    )(own_part, parts, out_weight)


def local(
    queries, fresh_span_keys, fresh_span_values, context_keys, context_values, selected, out_weight
):
    q_all, span_keys, span_values, pair_k, pair_v, own_part = gather(
        selected, queries, fresh_span_keys, fresh_span_values, context_keys, context_values
    )
    parts = attend(
        selected, q_all, span_keys, span_values, context_keys, context_values, pair_k, pair_v
    )
    return combine(own_part, parts, out_weight)


def solution(mesh):
    return jax.shard_map(
        local,
        mesh=mesh,
        in_specs=(
            P("ctx", "head"),
            P("ctx", "head"),
            P("ctx", "head"),
            P("ctx", "head"),
            P("ctx", "head"),
            P(),
            P("head", "ctx"),
        ),
        out_specs=P("head", "ctx"),
        check_vma=False,
    )
```

```python
import math

import jax
import jax.numpy as jnp
from jax import lax
from jax.experimental import pallas as pl
from jax.experimental.pallas import tpu as pltpu
from jax.sharding import PartitionSpec as P

HEAD_SIZE = 128
BLOCK_TOKENS = 4096
QUERY_BLOCK = 128
QUERY_BLOCKS = 4
PICKED = 12
SPAN = 512
NX, NY, NZ = 4, 8, 8
CORE_HEADS = 4
HALF = CORE_HEADS * HEAD_SIZE
WIDE = HALF + HEAD_SIZE
CHIP_TOKENS = 16
PART_ROWS = QUERY_BLOCK + CHIP_TOKENS
ROWS = CORE_HEADS * QUERY_BLOCK
KEY_PIECE = 1024
PIECES = BLOCK_TOKENS // KEY_PIECE
TILES = KEY_PIECE // HEAD_SIZE

EXP2_SCALE = math.log2(math.e) / math.sqrt(HEAD_SIZE)
NEG = -(2.0**100)
NEAR_FIRST = (1, 7, 2, 6, 3, 5, 4)
MESH = pl.DeviceIdType.MESH


def place():
    me = lax.axis_index("ctx")
    core = lax.rem(me, 2)
    chip = me // 2
    return me, chip // NY, lax.rem(chip, NY), core, lax.axis_index("head")


def greet(ids):
    barrier = pltpu.get_barrier_semaphore()
    for device in ids:
        pl.semaphore_signal(barrier, inc=1, device_id=device, device_id_type=MESH)
    pl.semaphore_wait(barrier, len(ids))


def remote(src, dst, send, recv, device):
    return pltpu.make_async_remote_copy(
        src_ref=src,
        dst_ref=dst,
        send_sem=send,
        recv_sem=recv,
        device_id=device,
        device_id_type=MESH,
    )


def stack_heads(qs, q_ref, start):
    for g in range(CORE_HEADS):
        qs[g * QUERY_BLOCK : (g + 1) * QUERY_BLOCK] = q_ref[
            pl.ds(start, QUERY_BLOCK), g * HEAD_SIZE : (g + 1) * HEAD_SIZE
        ]


def attend_span(chip, j, state, sk_ref, sv_ref):
    qs, m_s, l_s, acc_s = state
    s = lax.dot_general(
        qs[...], sk_ref[...], (((1,), (1,)), ((), ())), preferred_element_type=jnp.float32
    )
    token = j * QUERY_BLOCK + lax.rem(lax.broadcasted_iota(jnp.int32, s.shape, 0), QUERY_BLOCK)
    key = chip * CHIP_TOKENS + lax.broadcasted_iota(jnp.int32, s.shape, 1)
    keep = key <= token
    s = jnp.where(keep, s, NEG)
    m = jnp.max(s, axis=1, keepdims=True)
    p = jnp.where(keep, jnp.exp2((s - m) * EXP2_SCALE), 0.0)
    m_s[...] = jnp.broadcast_to(m, m_s.shape)
    l_s[...] = jnp.broadcast_to(jnp.sum(p, axis=1, keepdims=True), l_s.shape)
    acc_s[...] = jnp.dot(p.astype(jnp.bfloat16), sv_ref[...], preferred_element_type=jnp.float32)


def attend_block(b, state, kbuf, vbuf, s_buf, top_buf, hide=None):
    qs, m_s, l_s, acc_s = state

    def score(n):
        keys = kbuf[b, n * KEY_PIECE : (n + 1) * KEY_PIECE, :]
        scores = lax.dot_general(
            qs[...], keys, (((1,), (1,)), ((), ())), preferred_element_type=jnp.float32
        )
        s_buf[n % 2] = scores
        top = scores[:, :HEAD_SIZE]
        for t in range(1, TILES):
            top = jnp.maximum(top, scores[:, t * HEAD_SIZE : (t + 1) * HEAD_SIZE])
        top_buf[n % 2] = top

    def weigh(n):
        m_old = m_s[...]
        top = jnp.max(top_buf[n % 2], axis=1, keepdims=True)
        if hide is not None:
            top = top - hide
        m_new = jnp.maximum(m_old, top)
        shrink = jnp.exp2((m_old - m_new) * EXP2_SCALE)
        m_s[...] = m_new
        shift = m_new if hide is None else m_new + hide
        parts = []
        for t in range(TILES):
            part = jnp.exp2(
                (s_buf[n % 2, :, t * HEAD_SIZE : (t + 1) * HEAD_SIZE] - shift) * EXP2_SCALE
            )
            parts.append(part.astype(jnp.bfloat16))
        both = jnp.dot(
            jnp.concatenate(parts, axis=1),
            vbuf[b, n * KEY_PIECE : (n + 1) * KEY_PIECE, :],
            preferred_element_type=jnp.float32,
        )
        acc_s[...] = acc_s[...] * shrink + both[:, :HEAD_SIZE]
        l_s[...] = l_s[...] * shrink + both[:, HEAD_SIZE:]

    score(0)
    for n in range(PIECES):
        if n + 1 < PIECES:
            score(n + 1)
        weigh(n)


def store_partial(out_ref, state):
    _, m_s, l_s, acc_s = state
    stat_lane = lax.broadcasted_iota(jnp.int32, (QUERY_BLOCK, HEAD_SIZE), 1)
    m = m_s[...]
    m_sent = m.astype(jnp.bfloat16).astype(jnp.float32)
    grow = jnp.exp2((m - m_sent) * EXP2_SCALE)
    total = l_s[...] * grow
    high = total.astype(jnp.bfloat16).astype(jnp.float32)
    low = total - high
    acc = acc_s[...] * grow
    stats = jnp.zeros((QUERY_BLOCK, HEAD_SIZE), jnp.float32)
    for g in range(CORE_HEADS):
        here = slice(g * QUERY_BLOCK, (g + 1) * QUERY_BLOCK)
        out_ref[:QUERY_BLOCK, g * HEAD_SIZE : (g + 1) * HEAD_SIZE] = acc[here].astype(jnp.bfloat16)
        stats = jnp.where(stat_lane == g, m_sent[here], stats)
        stats = jnp.where(stat_lane == CORE_HEADS + g, high[here], stats)
        stats = jnp.where(stat_lane == 2 * CORE_HEADS + g, low[here], stats)
    packed = stats[:CHIP_TOKENS]
    for n in range(1, NY):
        packed = packed + pltpu.roll(
            stats[n * CHIP_TOKENS : (n + 1) * CHIP_TOKENS], n * CHIP_TOKENS, axis=1
        )
    out_ref[QUERY_BLOCK:, :HEAD_SIZE] = packed.astype(jnp.bfloat16)


def is_wanted(sel_ref, j, block):
    wanted = sel_ref[j, 0] == block
    for n in range(1, PICKED):
        wanted = jnp.logical_or(wanted, sel_ref[j, n] == block)
    return wanted


def attention_scratch():
    f32 = jnp.float32
    return [
        pltpu.VMEM((2, BLOCK_TOKENS, HEAD_SIZE), jnp.bfloat16),
        pltpu.VMEM((2, BLOCK_TOKENS, 2 * HEAD_SIZE), jnp.bfloat16),
        pltpu.VMEM((ROWS, HEAD_SIZE), jnp.bfloat16),
        pltpu.VMEM((ROWS, HEAD_SIZE), f32),
        pltpu.VMEM((ROWS, HEAD_SIZE), f32),
        pltpu.VMEM((ROWS, HEAD_SIZE), f32),
        pltpu.VMEM((2, ROWS, KEY_PIECE), f32),
        pltpu.VMEM((2, ROWS, HEAD_SIZE), f32),
    ]


def gather_kernel(
    sel_ref,
    q_ref,
    fk_ref,
    fv_ref,
    ck_ref,
    cv_ref,
    qall_ref,
    sk_ref,
    sv_ref,
    pk_ref,
    pv_ref,
    part_ref,
    kbuf,
    vbuf,
    qs,
    m_s,
    l_s,
    acc_s,
    s_buf,
    top_buf,
    q_own,
    sk_own,
    sv_own,
    part_own,
    load_sem,
    own_sem,
    pair_send,
    pair_recv,
    y_send,
    y_recv,
    x_send,
    x_recv,
):
    me, x, y, core, z = place()
    chip = me // 2
    other = me + 1 - 2 * core

    def device(dx, dy, to=core):
        return ((lax.rem(x + dx, NX) * NY + lax.rem(y + dy, NY)) * 2 + to, z)

    def own_span(ref, at):
        return ref.at[pl.ds(pl.multiple_of(at * 8, 8), 8)]

    def share(dx, dy):
        return lax.rem(x + NX - dx, NX) * NY + lax.rem(y + NY - dy, NY)

    def chunk(dx, dy):
        at = pl.multiple_of(share(dx, dy) * CHIP_TOKENS, CHIP_TOKENS)
        return qall_ref.at[pl.ds(at, CHIP_TOKENS)]

    def slab(device_at):
        return qall_ref.at[pl.ds(pl.multiple_of(device_at * 8, 8), 8)]

    greet(
        [(other, z)]
        + [device(0, dy) for dy in range(1, NY)]
        + [device(0, dy, 1 - core) for dy in range(1, NY)]
        + [device(dx, 0) for dx in range(1, NX)]
    )

    own_half = q_ref.at[:, pl.ds(pl.multiple_of(core * HALF, HALF), HALF)]
    other_half = q_ref.at[:, pl.ds(pl.multiple_of((1 - core) * HALF, HALF), HALF)]
    pairs = [
        remote(src, dst, pair_send.at[n], pair_recv.at[n], (other, z))
        for n, (src, dst) in enumerate(
            (
                (other_half, slab(me)),
                (fk_ref, own_span(sk_ref, core)),
                (fv_ref, own_span(sv_ref, core)),
                (ck_ref, pk_ref),
                (cv_ref, pv_ref),
            )
        )
    ]
    owns = [
        pltpu.make_async_copy(src, dst, own_sem.at[n])
        for n, (src, dst) in enumerate(
            (
                (own_half, slab(me)),
                (fk_ref, own_span(sk_ref, core)),
                (fv_ref, own_span(sv_ref, core)),
            )
        )
    ]
    pairs[0].start()
    for copy in owns:
        copy.start()
    sends = []
    for dy in (4, 3, 5, 2, 6, 1, 7):
        for side, (src, to) in enumerate(((own_half, core), (other_half, 1 - core))):
            copy = remote(
                src, slab(me), y_send.at[side, dy], y_recv.at[side, dy], device(0, dy, to)
            )
            copy.start()
            sends.append(copy)
    for copy in pairs[1:]:
        copy.start()

    def load(n, src, dst):
        return pltpu.make_async_copy(src, dst, load_sem.at[n])

    values = pl.ds(0, HEAD_SIZE)
    loads = [
        load(0, ck_ref, kbuf.at[0]),
        load(1, cv_ref, vbuf.at[0, :, values]),
        load(2, pk_ref, kbuf.at[1]),
        load(3, pv_ref, vbuf.at[1, :, values]),
        load(4, qall_ref.at[pl.ds(pl.multiple_of(x * QUERY_BLOCK, QUERY_BLOCK), QUERY_BLOCK)], q_own),
        load(5, sk_ref, sk_own),
        load(6, sv_ref, sv_own),
    ]
    loads[0].start()
    loads[1].start()
    vbuf[:, :, HEAD_SIZE:] = jnp.ones((2, BLOCK_TOKENS, HEAD_SIZE), jnp.bfloat16)
    owns[0].wait()
    remote(
        other_half, slab(other), pair_send.at[0], pair_recv.at[0], (other, z)
    ).wait_recv()

    def along_x(dx, dy):
        copy = remote(
            chunk(0, dy), chunk(0, dy), x_send.at[dx, dy], x_recv.at[dx, dy], device(dx, 0)
        )
        copy.start()
        sends.append(copy)

    for dx in (2, 1, 3):
        along_x(dx, 0)
    for dy in NEAR_FIRST:
        for side, at in enumerate((core, 1 - core)):
            spot = slab(share(0, dy) * 2 + at)
            remote(
                own_half, spot, y_send.at[side, dy], y_recv.at[side, dy], device(0, dy)
            ).wait_recv()
        for dx in (2, 1, 3):
            along_x(dx, dy)
    loads[4].start()
    spots = (own_span(sk_ref, 1 - core), own_span(sv_ref, 1 - core), pk_ref, pv_ref)
    for n, spot in enumerate(spots):
        remote(spot, spot, pair_send.at[n + 1], pair_recv.at[n + 1], (other, z)).wait_recv()
    for copy in owns[1:]:
        copy.wait()
    for n in (5, 6, 2, 3):
        loads[n].start()
    for n in (4, 5, 6):
        loads[n].wait()

    state = (qs, m_s, l_s, acc_s)
    stack_heads(qs, q_own, 0)
    attend_span(chip, x, state, sk_own, sv_own)
    for n in range(4):
        loads[n].wait()

    @pl.loop(0, 2)
    def _(b):
        block = jnp.where(b == 0, me, other)
        hide = jnp.where(is_wanted(sel_ref, x, block), 0.0, -2.0 * NEG)
        attend_block(b, state, kbuf, vbuf, s_buf, top_buf, hide)

    store_partial(part_own, state)
    result = load(7, part_own, part_ref)
    result.start()

    for dy in (0,) + NEAR_FIRST:
        for dx in (1, 3, 2):
            remote(
                chunk(dx, dy), chunk(dx, dy), x_send.at[dx, dy], x_recv.at[dx, dy], device(dx, 0)
            ).wait_recv()
    for copy in sends + pairs:
        copy.wait_send()
    result.wait()


def gather(selected, queries, fresh_keys, fresh_values, cache_keys, cache_values):
    anywhere = pl.BlockSpec(memory_space=pl.ANY)
    bf16 = jnp.bfloat16
    dma = pltpu.SemaphoreType.DMA
    return pl.pallas_call(
        gather_kernel,
        out_shape=(
            jax.ShapeDtypeStruct((SPAN, HALF), bf16),
            jax.ShapeDtypeStruct((CHIP_TOKENS, HEAD_SIZE), bf16),
            jax.ShapeDtypeStruct((CHIP_TOKENS, HEAD_SIZE), bf16),
            jax.ShapeDtypeStruct((BLOCK_TOKENS, HEAD_SIZE), bf16),
            jax.ShapeDtypeStruct((BLOCK_TOKENS, HEAD_SIZE), bf16),
            jax.ShapeDtypeStruct((PART_ROWS, HALF), bf16),
        ),
        in_specs=[pl.BlockSpec(memory_space=pltpu.SMEM)] + [anywhere] * 5,
        out_specs=[anywhere] * 6,
        scratch_shapes=attention_scratch()
        + [
            pltpu.VMEM((QUERY_BLOCK, HALF), bf16),
            pltpu.VMEM((CHIP_TOKENS, HEAD_SIZE), bf16),
            pltpu.VMEM((CHIP_TOKENS, HEAD_SIZE), bf16),
            pltpu.VMEM((PART_ROWS, HALF), bf16),
            dma((8,)),
            dma((3,)),
            dma((5,)),
            dma((5,)),
            dma((2, NY)),
            dma((2, NY)),
            dma((NX, NY)),
            dma((NX, NY)),
        ],
        compiler_params=pltpu.CompilerParams(collective_id=0, has_side_effects=True),
        name="gather_spans",
    )(selected, queries, fresh_keys, fresh_values, cache_keys, cache_values)


def attend_kernel(
    sel_ref,
    q_ref,
    sk_ref,
    sv_ref,
    ck_ref,
    cv_ref,
    pk_ref,
    pv_ref,
    out_ref,
    kbuf,
    vbuf,
    qs,
    m_s,
    l_s,
    acc_s,
    s_buf,
    top_buf,
    sems,
):
    me, x, y, core, z = place()
    chip = me // 2
    state = (qs, m_s, l_s, acc_s)
    copies = [
        pltpu.make_async_copy(src, dst, sems.at[n])
        for n, (src, dst) in enumerate(
            (
                (ck_ref, kbuf.at[0]),
                (cv_ref, vbuf.at[0, :, pl.ds(0, HEAD_SIZE)]),
                (pk_ref, kbuf.at[1]),
                (pv_ref, vbuf.at[1, :, pl.ds(0, HEAD_SIZE)]),
            )
        )
    ]
    for copy in copies:
        copy.start()
    vbuf[:, :, HEAD_SIZE:] = jnp.ones((2, BLOCK_TOKENS, HEAD_SIZE), jnp.bfloat16)

    @pl.loop(1, QUERY_BLOCKS)
    def _(n):
        j = lax.rem(x + n, QUERY_BLOCKS)
        stack_heads(qs, q_ref, pl.multiple_of(j * QUERY_BLOCK, QUERY_BLOCK))
        m_s[...] = jnp.full_like(m_s, NEG)
        l_s[...] = jnp.zeros_like(l_s)
        acc_s[...] = jnp.zeros_like(acc_s)

        @pl.when(j > x)
        def _():
            attend_span(chip, j, state, sk_ref, sv_ref)

        @pl.loop(0, 2)
        def _(b):
            block = jnp.where(b == 0, me, me + 1 - 2 * core)
            for half in range(2):

                @pl.when(jnp.logical_and(n == 1, b == half))
                def _():
                    copies[2 * half].wait()
                    copies[2 * half + 1].wait()

            @pl.when(is_wanted(sel_ref, j, block))
            def _():
                attend_block(b, state, kbuf, vbuf, s_buf, top_buf)

        store_partial(out_ref.at[j], state)


def attend(selected, q_all, span_keys, span_values, own_k, own_v, pair_k, pair_v):
    anywhere = pl.BlockSpec(memory_space=pl.ANY)
    vmem = pl.BlockSpec(memory_space=pltpu.VMEM)
    return pl.pallas_call(
        attend_kernel,
        out_shape=jax.ShapeDtypeStruct((QUERY_BLOCKS, PART_ROWS, HALF), jnp.bfloat16),
        in_specs=[pl.BlockSpec(memory_space=pltpu.SMEM), vmem, vmem, vmem] + [anywhere] * 4,
        out_specs=vmem,
        scratch_shapes=attention_scratch() + [pltpu.SemaphoreType.DMA((4,))],
        name="attend_blocks",
    )(selected, q_all, span_keys, span_values, own_k, own_v, pair_k, pair_v)


def merge(pieces, stats):
    joined = []
    for g in range(CORE_HEADS):
        tops = [stat[:, g : g + 1] for stat in stats]
        top = tops[0]
        for one in tops[1:]:
            top = jnp.maximum(top, one)
        total = jnp.zeros_like(top)
        acc = None
        for piece, stat, one in zip(pieces, stats, tops):
            weight = jnp.exp2((one - top) * EXP2_SCALE)
            total = total + weight * (
                stat[:, CORE_HEADS + g : CORE_HEADS + g + 1]
                + stat[:, 2 * CORE_HEADS + g : 2 * CORE_HEADS + g + 1]
            )
            term = weight * piece[:, g * HEAD_SIZE : (g + 1) * HEAD_SIZE].astype(jnp.float32)
            acc = term if acc is None else acc + term
        joined.append((top, total, acc))
    return joined


def combine_kernel(
    own_part_ref,
    part_ref,
    w_ref,
    out_ref,
    own,
    from_x,
    from_xs,
    merged,
    from_y,
    rows,
    partial,
    from_z,
    own_sem,
    s_send,
    s_recv,
    x_send,
    x_recv,
    y_send,
    y_recv,
    ay_send,
    ay_recv,
    ax_send,
    ax_recv,
    c_send,
    c_recv,
    z_send,
    z_recv,
):
    me, x, y, core, z = place()
    other = me + 1 - 2 * core
    f32 = jnp.float32

    def device(dx, dy):
        return ((lax.rem(x + dx, NX) * NY + lax.rem(y + dy, NY)) * 2 + core, z)

    greet(
        [(other, z)]
        + [device(0, dy) for dy in range(1, NY)]
        + [device(dx, 0) for dx in range(1, NX)]
        + [(me, lax.rem(z + dz, NZ)) for dz in range(1, NZ)]
    )
    sends = []

    def turn(n):
        return 4 + (1 - 2 * lax.rem(n, 2)) * ((n + 1) // 2)

    def piece(dy):
        at = lax.rem(y + dy, NY)
        return at, pl.ds(pl.multiple_of(at * CHIP_TOKENS, CHIP_TOKENS), CHIP_TOKENS)

    mine = pltpu.make_async_copy(own_part_ref, own, own_sem)
    mine.start()

    def to_x(dx, dy):
        _, here = piece(dy)
        return remote(
            part_ref.at[lax.rem(x + dx, NX), here],
            from_x.at[dx, here],
            x_send.at[dx, dy],
            x_recv.at[dx, dy],
            device(dx, 0),
        )

    def to_y(dy):
        return remote(
            merged.at[lax.rem(y + dy, NY)],
            from_y.at[dy],
            y_send.at[dy],
            y_recv.at[dy],
            device(0, dy),
        )

    for dx in (2, 1, 3):
        copy = remote(
            part_ref.at[lax.rem(x + dx, NX), pl.ds(QUERY_BLOCK, CHIP_TOKENS), pl.ds(0, HEAD_SIZE)],
            from_xs.at[dx],
            s_send.at[dx],
            s_recv.at[dx],
            device(dx, 0),
        )
        copy.start()
        sends.append(copy)

    @pl.loop(0, NY)
    def _(n):
        for dx in (2, 1, 3):
            to_x(dx, turn(n)).start()

    mine.wait()
    for dx in range(1, NX):
        remote(
            from_xs.at[dx], from_xs.at[dx], s_send.at[dx], s_recv.at[dx], device(dx, 0)
        ).wait_recv()
    stat_lane = lax.broadcasted_iota(jnp.int32, (CHIP_TOKENS, HEAD_SIZE), 1)

    @pl.loop(0, NY)
    def _(n):
        dy = turn(n)
        at, here = piece(dy)
        for dx in range(1, NX):
            spot = from_x.at[dx, here]
            remote(spot, spot, x_send.at[dx, dy], x_recv.at[dx, dy], device(dx, 0)).wait_recv()
        back = lax.rem(NY - at, NY) * CHIP_TOKENS
        tiles = [own[QUERY_BLOCK:, :HEAD_SIZE]] + [from_xs[dx] for dx in range(1, NX)]
        joined = merge(
            [own[here, :]] + [from_x[dx, here, :] for dx in range(1, NX)],
            [pltpu.roll(tile.astype(f32), back, axis=1) for tile in tiles],
        )
        stats = jnp.zeros((CHIP_TOKENS, HEAD_SIZE), f32)
        for g, (top, total, acc) in enumerate(joined):
            high = total.astype(jnp.bfloat16).astype(f32)
            stats = jnp.where(stat_lane == g, top, stats)
            stats = jnp.where(stat_lane == CORE_HEADS + g, high, stats)
            stats = jnp.where(stat_lane == 2 * CORE_HEADS + g, total - high, stats)
            merged[at, :, g * HEAD_SIZE : (g + 1) * HEAD_SIZE] = acc.astype(jnp.bfloat16)
        merged[at, :, HALF:WIDE] = stats.astype(jnp.bfloat16)

        @pl.when(n > 0)
        def _():
            to_y(turn(n - 1)).start()

    for dy in range(1, NY):
        remote(
            from_y.at[dy], from_y.at[dy], y_send.at[dy], y_recv.at[dy], device(0, dy)
        ).wait_recv()
    pieces = [merged[y]] + [from_y[dy] for dy in range(1, NY)]
    joined = merge(pieces, [item[:, HALF:].astype(f32) for item in pieces])
    for g, (_, total, acc) in enumerate(joined):
        rows[x, core, y, :, g * HEAD_SIZE : (g + 1) * HEAD_SIZE] = (acc / total).astype(
            jnp.bfloat16
        )

    def spot(dx, dy):
        return rows.at[lax.rem(x + NX - dx, NX), core, lax.rem(y + NY - dy, NY)]

    for dy in (4, 3, 5, 2, 6, 1, 7):
        copy = remote(spot(0, 0), spot(0, 0), ay_send.at[dy], ay_recv.at[dy], device(0, dy))
        copy.start()
        sends.append(copy)
    for dy in (0,) + NEAR_FIRST:
        if dy:
            remote(
                spot(0, dy), spot(0, dy), ay_send.at[dy], ay_recv.at[dy], device(0, dy)
            ).wait_recv()
        for dx in (2, 1, 3):
            copy = remote(
                spot(0, dy), spot(0, dy), ax_send.at[dx, dy], ax_recv.at[dx, dy], device(dx, 0)
            )
            copy.start()
            sends.append(copy)
    def swap(dx):
        group = rows.at[lax.rem(x + NX - dx, NX), core]
        copy = remote(group, group, c_send.at[dx], c_recv.at[dx], (other, z))
        copy.start()
        sends.append(copy)

    def project(at, dx):
        group = rows.at[at, 1 - core]
        remote(group, group, c_send.at[dx], c_recv.at[dx], (other, z)).wait_recv()
        product = jnp.dot(
            rows[at, 0].reshape(QUERY_BLOCK, HALF), w_ref[:HALF, :], preferred_element_type=f32
        ) + jnp.dot(
            rows[at, 1].reshape(QUERY_BLOCK, HALF), w_ref[HALF:, :], preferred_element_type=f32
        )
        product = product.astype(jnp.bfloat16)
        for half in range(2):
            partial[2 * at + half] = product[half * 64 : (half + 1) * 64]
        for half in range(2):
            to = 2 * at + half

            @pl.when(to != z)
            def _():
                remote(
                    partial.at[to], from_z.at[z], z_send.at[to], z_recv.at[z], (me, to)
                ).start()

    swap(0)
    project(x, 0)
    for dx in (1, 3, 2):
        for dy in (0,) + NEAR_FIRST:
            remote(
                spot(dx, dy), spot(dx, dy), ax_send.at[dx, dy], ax_recv.at[dx, dy], device(dx, 0)
            ).wait_recv()
        swap(dx)

    @pl.loop(0, NX)
    def _(n):
        at = lax.rem(z // 2 + 2 + (1 - 2 * lax.rem(n, 2)) * ((n + 1) // 2), NX)

        @pl.when(at != x)
        def _():
            project(at, lax.rem(x + NX - at, NX))

    total = partial[z].astype(f32)
    for dz in range(1, NZ):
        source = lax.rem(z + dz, NZ)
        copy = remote(
            partial.at[source], from_z.at[source], z_send.at[source], z_recv.at[source], (me, source)
        )
        copy.wait_send()
        copy.wait_recv()
        total = total + from_z[source].astype(f32)
    out_ref[...] = total.astype(jnp.bfloat16)

    @pl.loop(0, NY)
    def _(dy):
        for dx in range(1, NX):
            to_x(dx, dy).wait_send()

        @pl.when(dy > 0)
        def _():
            to_y(dy).wait_send()

    for copy in sends:
        copy.wait_send()


def combine(own_part, parts, out_weight):
    vmem = pl.BlockSpec(memory_space=pltpu.VMEM)
    bf16 = jnp.bfloat16
    dma = pltpu.SemaphoreType.DMA
    return pl.pallas_call(
        combine_kernel,
        out_shape=jax.ShapeDtypeStruct((SPAN // NZ, HEAD_SIZE), bf16),
        in_specs=[pl.BlockSpec(memory_space=pl.ANY)] * 2 + [vmem],
        out_specs=vmem,
        scratch_shapes=[
            pltpu.VMEM((PART_ROWS, HALF), bf16),
            pltpu.VMEM((NX, QUERY_BLOCK, HALF), bf16),
            pltpu.VMEM((NX, CHIP_TOKENS, HEAD_SIZE), bf16),
            pltpu.VMEM((NY, CHIP_TOKENS, WIDE), bf16),
            pltpu.VMEM((NY, CHIP_TOKENS, WIDE), bf16),
            pltpu.VMEM((NX, 2, NY, CHIP_TOKENS, HALF), bf16),
            pltpu.VMEM((NZ, SPAN // NZ, HEAD_SIZE), bf16),
            pltpu.VMEM((NZ, SPAN // NZ, HEAD_SIZE), bf16),
            dma,
            dma((NX,)),
            dma((NX,)),
            dma((NX, NY)),
            dma((NX, NY)),
            dma((NY,)),
            dma((NY,)),
            dma((NY,)),
            dma((NY,)),
            dma((NX, NY)),
            dma((NX, NY)),
            dma((NX,)),
            dma((NX,)),
            dma((NZ,)),
            dma((NZ,)),
        ],
        compiler_params=pltpu.CompilerParams(collective_id=1, has_side_effects=True),
        name="combine_rows",
    )(own_part, parts, out_weight)


def local(
    queries, fresh_span_keys, fresh_span_values, context_keys, context_values, selected, out_weight
):
    q_all, span_keys, span_values, pair_k, pair_v, own_part = gather(
        selected, queries, fresh_span_keys, fresh_span_values, context_keys, context_values
    )
    parts = attend(
        selected, q_all, span_keys, span_values, context_keys, context_values, pair_k, pair_v
    )
    return combine(own_part, parts, out_weight)


def solution(mesh):
    return jax.shard_map(
        local,
        mesh=mesh,
        in_specs=(
            P("ctx", "head"),
            P("ctx", "head"),
            P("ctx", "head"),
            P("ctx", "head"),
            P("ctx", "head"),
            P(),
            P("head", "ctx"),
        ),
        out_specs=P("head", "ctx"),
        check_vma=False,
    )
```

```python
import math

import jax
import jax.numpy as jnp
from jax import lax
from jax.experimental import pallas as pl
from jax.experimental.pallas import tpu as pltpu
from jax.sharding import PartitionSpec as P

HEAD_SIZE = 128
BLOCK_TOKENS = 4096
QUERY_BLOCK = 128
QUERY_BLOCKS = 4
PICKED = 12
SPAN = 512
NX, NY, NZ = 4, 8, 8
CORE_HEADS = 4
HALF = CORE_HEADS * HEAD_SIZE
WIDE = HALF + HEAD_SIZE
CHIP_TOKENS = 16
PART_ROWS = QUERY_BLOCK + CHIP_TOKENS
ROWS = CORE_HEADS * QUERY_BLOCK
KEY_PIECE = 1024
PIECES = BLOCK_TOKENS // KEY_PIECE
TILES = KEY_PIECE // HEAD_SIZE

EXP2_SCALE = math.log2(math.e) / math.sqrt(HEAD_SIZE)
NEG = -(2.0**100)
NEAR_FIRST = (1, 7, 2, 6, 3, 5, 4)
MESH = pl.DeviceIdType.MESH


def place():
    me = lax.axis_index("ctx")
    core = lax.rem(me, 2)
    chip = me // 2
    return me, chip // NY, lax.rem(chip, NY), core, lax.axis_index("head")


def greet(ids):
    barrier = pltpu.get_barrier_semaphore()
    for device in ids:
        pl.semaphore_signal(barrier, inc=1, device_id=device, device_id_type=MESH)
    pl.semaphore_wait(barrier, len(ids))


def remote(src, dst, send, recv, device):
    return pltpu.make_async_remote_copy(
        src_ref=src,
        dst_ref=dst,
        send_sem=send,
        recv_sem=recv,
        device_id=device,
        device_id_type=MESH,
    )


def stack_heads(qs, q_ref, start):
    for g in range(CORE_HEADS):
        qs[g * QUERY_BLOCK : (g + 1) * QUERY_BLOCK] = q_ref[
            pl.ds(start, QUERY_BLOCK), g * HEAD_SIZE : (g + 1) * HEAD_SIZE
        ]


def attend_span(chip, j, state, sk_ref, sv_ref):
    qs, m_s, l_s, acc_s = state
    s = lax.dot_general(
        qs[...], sk_ref[...], (((1,), (1,)), ((), ())), preferred_element_type=jnp.float32
    )
    token = j * QUERY_BLOCK + lax.rem(lax.broadcasted_iota(jnp.int32, s.shape, 0), QUERY_BLOCK)
    key = chip * CHIP_TOKENS + lax.broadcasted_iota(jnp.int32, s.shape, 1)
    keep = key <= token
    s = jnp.where(keep, s, NEG)
    m = jnp.max(s, axis=1, keepdims=True)
    p = jnp.where(keep, jnp.exp2((s - m) * EXP2_SCALE), 0.0)
    m_s[...] = jnp.broadcast_to(m, m_s.shape)
    l_s[...] = jnp.broadcast_to(jnp.sum(p, axis=1, keepdims=True), l_s.shape)
    acc_s[...] = jnp.dot(p.astype(jnp.bfloat16), sv_ref[...], preferred_element_type=jnp.float32)


def attend_block(b, state, kbuf, vbuf, s_buf, top_buf, hide=None):
    qs, m_s, l_s, acc_s = state

    def score(n):
        keys = kbuf[b, n * KEY_PIECE : (n + 1) * KEY_PIECE, :]
        scores = lax.dot_general(
            qs[...], keys, (((1,), (1,)), ((), ())), preferred_element_type=jnp.float32
        )
        s_buf[n % 2] = scores
        top = scores[:, :HEAD_SIZE]
        for t in range(1, TILES):
            top = jnp.maximum(top, scores[:, t * HEAD_SIZE : (t + 1) * HEAD_SIZE])
        top_buf[n % 2] = top

    def weigh(n):
        m_old = m_s[...]
        top = jnp.max(top_buf[n % 2], axis=1, keepdims=True)
        if hide is not None:
            top = top - hide
        m_new = jnp.maximum(m_old, top)
        shrink = jnp.exp2((m_old - m_new) * EXP2_SCALE)
        m_s[...] = m_new
        shift = m_new if hide is None else m_new + hide
        parts = []
        for t in range(TILES):
            part = jnp.exp2(
                (s_buf[n % 2, :, t * HEAD_SIZE : (t + 1) * HEAD_SIZE] - shift) * EXP2_SCALE
            )
            parts.append(part.astype(jnp.bfloat16))
        both = jnp.dot(
            jnp.concatenate(parts, axis=1),
            vbuf[b, n * KEY_PIECE : (n + 1) * KEY_PIECE, :],
            preferred_element_type=jnp.float32,
        )
        acc_s[...] = acc_s[...] * shrink + both[:, :HEAD_SIZE]
        l_s[...] = l_s[...] * shrink + both[:, HEAD_SIZE:]

    score(0)
    for n in range(PIECES):
        if n + 1 < PIECES:
            score(n + 1)
        weigh(n)


def store_partial(out_ref, state):
    _, m_s, l_s, acc_s = state
    stat_lane = lax.broadcasted_iota(jnp.int32, (QUERY_BLOCK, HEAD_SIZE), 1)
    m = m_s[...]
    m_sent = m.astype(jnp.bfloat16).astype(jnp.float32)
    grow = jnp.exp2((m - m_sent) * EXP2_SCALE)
    total = l_s[...] * grow
    high = total.astype(jnp.bfloat16).astype(jnp.float32)
    low = total - high
    acc = acc_s[...] * grow
    stats = jnp.zeros((QUERY_BLOCK, HEAD_SIZE), jnp.float32)
    for g in range(CORE_HEADS):
        here = slice(g * QUERY_BLOCK, (g + 1) * QUERY_BLOCK)
        out_ref[:QUERY_BLOCK, g * HEAD_SIZE : (g + 1) * HEAD_SIZE] = acc[here].astype(jnp.bfloat16)
        stats = jnp.where(stat_lane == g, m_sent[here], stats)
        stats = jnp.where(stat_lane == CORE_HEADS + g, high[here], stats)
        stats = jnp.where(stat_lane == 2 * CORE_HEADS + g, low[here], stats)
    packed = stats[:CHIP_TOKENS]
    for n in range(1, NY):
        packed = packed + pltpu.roll(
            stats[n * CHIP_TOKENS : (n + 1) * CHIP_TOKENS], n * CHIP_TOKENS, axis=1
        )
    out_ref[QUERY_BLOCK:, :HEAD_SIZE] = packed.astype(jnp.bfloat16)


def is_wanted(sel_ref, j, block):
    wanted = sel_ref[j, 0] == block
    for n in range(1, PICKED):
        wanted = jnp.logical_or(wanted, sel_ref[j, n] == block)
    return wanted


def attention_scratch():
    f32 = jnp.float32
    return [
        pltpu.VMEM((2, BLOCK_TOKENS, HEAD_SIZE), jnp.bfloat16),
        pltpu.VMEM((2, BLOCK_TOKENS, 2 * HEAD_SIZE), jnp.bfloat16),
        pltpu.VMEM((ROWS, HEAD_SIZE), jnp.bfloat16),
        pltpu.VMEM((ROWS, HEAD_SIZE), f32),
        pltpu.VMEM((ROWS, HEAD_SIZE), f32),
        pltpu.VMEM((ROWS, HEAD_SIZE), f32),
        pltpu.VMEM((2, ROWS, KEY_PIECE), f32),
        pltpu.VMEM((2, ROWS, HEAD_SIZE), f32),
    ]


def gather_kernel(
    sel_ref,
    q_ref,
    fk_ref,
    fv_ref,
    ck_ref,
    cv_ref,
    qall_ref,
    sk_ref,
    sv_ref,
    pk_ref,
    pv_ref,
    part_ref,
    kbuf,
    vbuf,
    qs,
    m_s,
    l_s,
    acc_s,
    s_buf,
    top_buf,
    q_own,
    sk_own,
    sv_own,
    part_own,
    load_sem,
    own_sem,
    pair_send,
    pair_recv,
    y_send,
    y_recv,
    x_send,
    x_recv,
):
    me, x, y, core, z = place()
    chip = me // 2
    other = me + 1 - 2 * core

    def device(dx, dy, to=core):
        return ((lax.rem(x + dx, NX) * NY + lax.rem(y + dy, NY)) * 2 + to, z)

    def own_span(ref, at):
        return ref.at[pl.ds(pl.multiple_of(at * 8, 8), 8)]

    def share(dx, dy):
        return lax.rem(x + NX - dx, NX) * NY + lax.rem(y + NY - dy, NY)

    def chunk(dx, dy):
        at = pl.multiple_of(share(dx, dy) * CHIP_TOKENS, CHIP_TOKENS)
        return qall_ref.at[pl.ds(at, CHIP_TOKENS)]

    def slab(device_at):
        return qall_ref.at[pl.ds(pl.multiple_of(device_at * 8, 8), 8)]

    greet(
        [(other, z)]
        + [device(0, dy) for dy in range(1, NY)]
        + [device(0, dy, 1 - core) for dy in range(1, NY)]
        + [device(dx, 0) for dx in range(1, NX)]
    )

    own_half = q_ref.at[:, pl.ds(pl.multiple_of(core * HALF, HALF), HALF)]
    other_half = q_ref.at[:, pl.ds(pl.multiple_of((1 - core) * HALF, HALF), HALF)]
    pairs = [
        remote(src, dst, pair_send.at[n], pair_recv.at[n], (other, z))
        for n, (src, dst) in enumerate(
            (
                (other_half, slab(me)),
                (fk_ref, own_span(sk_ref, core)),
                (fv_ref, own_span(sv_ref, core)),
                (ck_ref, pk_ref),
                (cv_ref, pv_ref),
            )
        )
    ]
    owns = [
        pltpu.make_async_copy(src, dst, own_sem.at[n])
        for n, (src, dst) in enumerate(
            (
                (own_half, slab(me)),
                (fk_ref, own_span(sk_ref, core)),
                (fv_ref, own_span(sv_ref, core)),
            )
        )
    ]
    pairs[0].start()
    for copy in owns:
        copy.start()
    sends = []
    for dy in (4, 3, 5, 2, 6, 1, 7):
        for side, (src, to) in enumerate(((own_half, core), (other_half, 1 - core))):
            copy = remote(
                src, slab(me), y_send.at[side, dy], y_recv.at[side, dy], device(0, dy, to)
            )
            copy.start()
            sends.append(copy)
    for copy in pairs[1:]:
        copy.start()

    def load(n, src, dst):
        return pltpu.make_async_copy(src, dst, load_sem.at[n])

    values = pl.ds(0, HEAD_SIZE)
    loads = [
        load(0, ck_ref, kbuf.at[0]),
        load(1, cv_ref, vbuf.at[0, :, values]),
        load(2, pk_ref, kbuf.at[1]),
        load(3, pv_ref, vbuf.at[1, :, values]),
        load(4, qall_ref.at[pl.ds(pl.multiple_of(x * QUERY_BLOCK, QUERY_BLOCK), QUERY_BLOCK)], q_own),
        load(5, sk_ref, sk_own),
        load(6, sv_ref, sv_own),
    ]
    loads[0].start()
    loads[1].start()
    vbuf[:, :, HEAD_SIZE:] = jnp.ones((2, BLOCK_TOKENS, HEAD_SIZE), jnp.bfloat16)
    owns[0].wait()
    remote(
        other_half, slab(other), pair_send.at[0], pair_recv.at[0], (other, z)
    ).wait_recv()

    def along_x(dx, dy):
        copy = remote(
            chunk(0, dy), chunk(0, dy), x_send.at[dx, dy], x_recv.at[dx, dy], device(dx, 0)
        )
        copy.start()
        sends.append(copy)

    for dx in (2, 1, 3):
        along_x(dx, 0)
    for dy in NEAR_FIRST:
        for side, at in enumerate((core, 1 - core)):
            spot = slab(share(0, dy) * 2 + at)
            remote(
                own_half, spot, y_send.at[side, dy], y_recv.at[side, dy], device(0, dy)
            ).wait_recv()
        for dx in (2, 1, 3):
            along_x(dx, dy)
    loads[4].start()
    spots = (own_span(sk_ref, 1 - core), own_span(sv_ref, 1 - core), pk_ref, pv_ref)
    for n, spot in enumerate(spots):
        remote(spot, spot, pair_send.at[n + 1], pair_recv.at[n + 1], (other, z)).wait_recv()
    for copy in owns[1:]:
        copy.wait()
    for n in (5, 6, 2, 3):
        loads[n].start()
    for n in (4, 5, 6):
        loads[n].wait()

    state = (qs, m_s, l_s, acc_s)
    stack_heads(qs, q_own, 0)
    attend_span(chip, x, state, sk_own, sv_own)
    for n in range(4):
        loads[n].wait()

    @pl.loop(0, 2)
    def _(b):
        block = jnp.where(b == 0, me, other)
        hide = jnp.where(is_wanted(sel_ref, x, block), 0.0, -2.0 * NEG)
        attend_block(b, state, kbuf, vbuf, s_buf, top_buf, hide)

    store_partial(part_own, state)
    result = load(7, part_own, part_ref)
    result.start()

    for dy in (0,) + NEAR_FIRST:
        for dx in (1, 3, 2):
            remote(
                chunk(dx, dy), chunk(dx, dy), x_send.at[dx, dy], x_recv.at[dx, dy], device(dx, 0)
            ).wait_recv()
    for copy in sends + pairs:
        copy.wait_send()
    result.wait()


def gather(selected, queries, fresh_keys, fresh_values, cache_keys, cache_values):
    anywhere = pl.BlockSpec(memory_space=pl.ANY)
    bf16 = jnp.bfloat16
    dma = pltpu.SemaphoreType.DMA
    return pl.pallas_call(
        gather_kernel,
        out_shape=(
            jax.ShapeDtypeStruct((SPAN, HALF), bf16),
            jax.ShapeDtypeStruct((CHIP_TOKENS, HEAD_SIZE), bf16),
            jax.ShapeDtypeStruct((CHIP_TOKENS, HEAD_SIZE), bf16),
            jax.ShapeDtypeStruct((BLOCK_TOKENS, HEAD_SIZE), bf16),
            jax.ShapeDtypeStruct((BLOCK_TOKENS, HEAD_SIZE), bf16),
            jax.ShapeDtypeStruct((PART_ROWS, HALF), bf16),
        ),
        in_specs=[pl.BlockSpec(memory_space=pltpu.SMEM)] + [anywhere] * 5,
        out_specs=[anywhere] * 6,
        scratch_shapes=attention_scratch()
        + [
            pltpu.VMEM((QUERY_BLOCK, HALF), bf16),
            pltpu.VMEM((CHIP_TOKENS, HEAD_SIZE), bf16),
            pltpu.VMEM((CHIP_TOKENS, HEAD_SIZE), bf16),
            pltpu.VMEM((PART_ROWS, HALF), bf16),
            dma((8,)),
            dma((3,)),
            dma((5,)),
            dma((5,)),
            dma((2, NY)),
            dma((2, NY)),
            dma((NX, NY)),
            dma((NX, NY)),
        ],
        compiler_params=pltpu.CompilerParams(collective_id=0, has_side_effects=True),
        name="gather_spans",
    )(selected, queries, fresh_keys, fresh_values, cache_keys, cache_values)


def attend_kernel(
    sel_ref,
    q_ref,
    sk_ref,
    sv_ref,
    ck_ref,
    cv_ref,
    pk_ref,
    pv_ref,
    out_ref,
    kbuf,
    vbuf,
    qs,
    m_s,
    l_s,
    acc_s,
    s_buf,
    top_buf,
    sems,
):
    me, x, y, core, z = place()
    chip = me // 2
    state = (qs, m_s, l_s, acc_s)
    copies = [
        pltpu.make_async_copy(src, dst, sems.at[n])
        for n, (src, dst) in enumerate(
            (
                (ck_ref, kbuf.at[0]),
                (cv_ref, vbuf.at[0, :, pl.ds(0, HEAD_SIZE)]),
                (pk_ref, kbuf.at[1]),
                (pv_ref, vbuf.at[1, :, pl.ds(0, HEAD_SIZE)]),
            )
        )
    ]
    for copy in copies:
        copy.start()
    vbuf[:, :, HEAD_SIZE:] = jnp.ones((2, BLOCK_TOKENS, HEAD_SIZE), jnp.bfloat16)

    @pl.loop(1, QUERY_BLOCKS)
    def _(n):
        j = lax.rem(x + n, QUERY_BLOCKS)
        stack_heads(qs, q_ref, pl.multiple_of(j * QUERY_BLOCK, QUERY_BLOCK))
        m_s[...] = jnp.full_like(m_s, NEG)
        l_s[...] = jnp.zeros_like(l_s)
        acc_s[...] = jnp.zeros_like(acc_s)

        @pl.when(j > x)
        def _():
            attend_span(chip, j, state, sk_ref, sv_ref)

        @pl.loop(0, 2)
        def _(b):
            block = jnp.where(b == 0, me, me + 1 - 2 * core)
            for half in range(2):

                @pl.when(jnp.logical_and(n == 1, b == half))
                def _():
                    copies[2 * half].wait()
                    copies[2 * half + 1].wait()

            @pl.when(is_wanted(sel_ref, j, block))
            def _():
                attend_block(b, state, kbuf, vbuf, s_buf, top_buf)

        store_partial(out_ref.at[j], state)


def attend(selected, q_all, span_keys, span_values, own_k, own_v, pair_k, pair_v):
    anywhere = pl.BlockSpec(memory_space=pl.ANY)
    vmem = pl.BlockSpec(memory_space=pltpu.VMEM)
    return pl.pallas_call(
        attend_kernel,
        out_shape=jax.ShapeDtypeStruct((QUERY_BLOCKS, PART_ROWS, HALF), jnp.bfloat16),
        in_specs=[pl.BlockSpec(memory_space=pltpu.SMEM), vmem, vmem, vmem] + [anywhere] * 4,
        out_specs=vmem,
        scratch_shapes=attention_scratch() + [pltpu.SemaphoreType.DMA((4,))],
        name="attend_blocks",
    )(selected, q_all, span_keys, span_values, own_k, own_v, pair_k, pair_v)


def merge(pieces, stats):
    joined = []
    for g in range(CORE_HEADS):
        tops = [stat[:, g : g + 1] for stat in stats]
        top = tops[0]
        for one in tops[1:]:
            top = jnp.maximum(top, one)
        total = jnp.zeros_like(top)
        acc = None
        for piece, stat, one in zip(pieces, stats, tops):
            weight = jnp.exp2((one - top) * EXP2_SCALE)
            total = total + weight * (
                stat[:, CORE_HEADS + g : CORE_HEADS + g + 1]
                + stat[:, 2 * CORE_HEADS + g : 2 * CORE_HEADS + g + 1]
            )
            term = weight * piece[:, g * HEAD_SIZE : (g + 1) * HEAD_SIZE].astype(jnp.float32)
            acc = term if acc is None else acc + term
        joined.append((top, total, acc))
    return joined


def combine_kernel(
    own_part_ref,
    part_ref,
    w_ref,
    out_ref,
    own,
    from_x,
    from_xs,
    merged,
    from_y,
    rows,
    partial,
    from_z,
    own_sem,
    s_send,
    s_recv,
    x_send,
    x_recv,
    y_send,
    y_recv,
    ay_send,
    ay_recv,
    ax_send,
    ax_recv,
    c_send,
    c_recv,
    z_send,
    z_recv,
):
    me, x, y, core, z = place()
    other = me + 1 - 2 * core
    f32 = jnp.float32

    def device(dx, dy):
        return ((lax.rem(x + dx, NX) * NY + lax.rem(y + dy, NY)) * 2 + core, z)

    greet(
        [(other, z)]
        + [device(0, dy) for dy in range(1, NY)]
        + [device(dx, 0) for dx in range(1, NX)]
        + [(me, lax.rem(z + dz, NZ)) for dz in range(1, NZ)]
    )
    sends = []

    def turn(n):
        return 4 + (1 - 2 * lax.rem(n, 2)) * ((n + 1) // 2)

    def piece(dy):
        at = lax.rem(y + dy, NY)
        return at, pl.ds(pl.multiple_of(at * CHIP_TOKENS, CHIP_TOKENS), CHIP_TOKENS)

    mine = pltpu.make_async_copy(own_part_ref, own, own_sem)
    mine.start()

    def to_x(dx, dy):
        _, here = piece(dy)
        return remote(
            part_ref.at[lax.rem(x + dx, NX), here],
            from_x.at[dx, here],
            x_send.at[dx, dy],
            x_recv.at[dx, dy],
            device(dx, 0),
        )

    def to_y(dy):
        return remote(
            merged.at[lax.rem(y + dy, NY)],
            from_y.at[dy],
            y_send.at[dy],
            y_recv.at[dy],
            device(0, dy),
        )

    for dx in (2, 1, 3):
        copy = remote(
            part_ref.at[lax.rem(x + dx, NX), pl.ds(QUERY_BLOCK, CHIP_TOKENS), pl.ds(0, HEAD_SIZE)],
            from_xs.at[dx],
            s_send.at[dx],
            s_recv.at[dx],
            device(dx, 0),
        )
        copy.start()
        sends.append(copy)

    @pl.loop(0, NY)
    def _(n):
        for dx in (2, 1, 3):
            to_x(dx, turn(n)).start()

    mine.wait()
    for dx in range(1, NX):
        remote(
            from_xs.at[dx], from_xs.at[dx], s_send.at[dx], s_recv.at[dx], device(dx, 0)
        ).wait_recv()
    stat_lane = lax.broadcasted_iota(jnp.int32, (CHIP_TOKENS, HEAD_SIZE), 1)

    @pl.loop(0, NY)
    def _(n):
        dy = turn(n)
        at, here = piece(dy)
        for dx in range(1, NX):
            spot = from_x.at[dx, here]
            remote(spot, spot, x_send.at[dx, dy], x_recv.at[dx, dy], device(dx, 0)).wait_recv()
        back = lax.rem(NY - at, NY) * CHIP_TOKENS
        tiles = [own[QUERY_BLOCK:, :HEAD_SIZE]] + [from_xs[dx] for dx in range(1, NX)]
        joined = merge(
            [own[here, :]] + [from_x[dx, here, :] for dx in range(1, NX)],
            [pltpu.roll(tile.astype(f32), back, axis=1) for tile in tiles],
        )
        stats = jnp.zeros((CHIP_TOKENS, HEAD_SIZE), f32)
        for g, (top, total, acc) in enumerate(joined):
            high = total.astype(jnp.bfloat16).astype(f32)
            stats = jnp.where(stat_lane == g, top, stats)
            stats = jnp.where(stat_lane == CORE_HEADS + g, high, stats)
            stats = jnp.where(stat_lane == 2 * CORE_HEADS + g, total - high, stats)
            merged[at, :, g * HEAD_SIZE : (g + 1) * HEAD_SIZE] = acc.astype(jnp.bfloat16)
        merged[at, :, HALF:WIDE] = stats.astype(jnp.bfloat16)

        @pl.when(n > 0)
        def _():
            to_y(turn(n - 1)).start()

    for dy in range(1, NY):
        remote(
            from_y.at[dy], from_y.at[dy], y_send.at[dy], y_recv.at[dy], device(0, dy)
        ).wait_recv()
    pieces = [merged[y]] + [from_y[dy] for dy in range(1, NY)]
    joined = merge(pieces, [item[:, HALF:].astype(f32) for item in pieces])
    for g, (_, total, acc) in enumerate(joined):
        rows[x, core, y, :, g * HEAD_SIZE : (g + 1) * HEAD_SIZE] = (acc / total).astype(
            jnp.bfloat16
        )

    def spot(dx, dy):
        return rows.at[lax.rem(x + NX - dx, NX), core, lax.rem(y + NY - dy, NY)]

    for dy in (4, 3, 5, 2, 6, 1, 7):
        copy = remote(spot(0, 0), spot(0, 0), ay_send.at[dy], ay_recv.at[dy], device(0, dy))
        copy.start()
        sends.append(copy)
    for dy in (0,) + NEAR_FIRST:
        if dy:
            remote(
                spot(0, dy), spot(0, dy), ay_send.at[dy], ay_recv.at[dy], device(0, dy)
            ).wait_recv()
        for dx in (2, 1, 3):
            copy = remote(
                spot(0, dy), spot(0, dy), ax_send.at[dx, dy], ax_recv.at[dx, dy], device(dx, 0)
            )
            copy.start()
            sends.append(copy)
    def swap(dx):
        group = rows.at[lax.rem(x + NX - dx, NX), core]
        copy = remote(group, group, c_send.at[dx], c_recv.at[dx], (other, z))
        copy.start()
        sends.append(copy)

    def project(at, dx):
        group = rows.at[at, 1 - core]
        remote(group, group, c_send.at[dx], c_recv.at[dx], (other, z)).wait_recv()
        product = jnp.dot(
            rows[at, 0].reshape(QUERY_BLOCK, HALF), w_ref[:HALF, :], preferred_element_type=f32
        ) + jnp.dot(
            rows[at, 1].reshape(QUERY_BLOCK, HALF), w_ref[HALF:, :], preferred_element_type=f32
        )
        product = product.astype(jnp.bfloat16)
        for half in range(2):
            partial[2 * at + half] = product[half * 64 : (half + 1) * 64]
        for half in range(2):
            to = 2 * at + half

            @pl.when(to != z)
            def _():
                remote(
                    partial.at[to], from_z.at[z], z_send.at[to], z_recv.at[z], (me, to)
                ).start()

    swap(0)
    project(x, 0)
    for dx in (1, 3, 2):
        for dy in (0,) + NEAR_FIRST:
            remote(
                spot(dx, dy), spot(dx, dy), ax_send.at[dx, dy], ax_recv.at[dx, dy], device(dx, 0)
            ).wait_recv()
        swap(dx)
    for dx in (1, 3, 2):
        project(lax.rem(x + NX - dx, NX), dx)

    total = partial[z].astype(f32)
    for dz in range(1, NZ):
        source = lax.rem(z + dz, NZ)
        copy = remote(
            partial.at[source], from_z.at[source], z_send.at[source], z_recv.at[source], (me, source)
        )
        copy.wait_send()
        copy.wait_recv()
        total = total + from_z[source].astype(f32)
    out_ref[...] = total.astype(jnp.bfloat16)

    @pl.loop(0, NY)
    def _(dy):
        for dx in range(1, NX):
            to_x(dx, dy).wait_send()

        @pl.when(dy > 0)
        def _():
            to_y(dy).wait_send()

    for copy in sends:
        copy.wait_send()


def combine(own_part, parts, out_weight):
    vmem = pl.BlockSpec(memory_space=pltpu.VMEM)
    bf16 = jnp.bfloat16
    dma = pltpu.SemaphoreType.DMA
    return pl.pallas_call(
        combine_kernel,
        out_shape=jax.ShapeDtypeStruct((SPAN // NZ, HEAD_SIZE), bf16),
        in_specs=[pl.BlockSpec(memory_space=pl.ANY)] * 2 + [vmem],
        out_specs=vmem,
        scratch_shapes=[
            pltpu.VMEM((PART_ROWS, HALF), bf16),
            pltpu.VMEM((NX, QUERY_BLOCK, HALF), bf16),
            pltpu.VMEM((NX, CHIP_TOKENS, HEAD_SIZE), bf16),
            pltpu.VMEM((NY, CHIP_TOKENS, WIDE), bf16),
            pltpu.VMEM((NY, CHIP_TOKENS, WIDE), bf16),
            pltpu.VMEM((NX, 2, NY, CHIP_TOKENS, HALF), bf16),
            pltpu.VMEM((NZ, SPAN // NZ, HEAD_SIZE), bf16),
            pltpu.VMEM((NZ, SPAN // NZ, HEAD_SIZE), bf16),
            dma,
            dma((NX,)),
            dma((NX,)),
            dma((NX, NY)),
            dma((NX, NY)),
            dma((NY,)),
            dma((NY,)),
            dma((NY,)),
            dma((NY,)),
            dma((NX, NY)),
            dma((NX, NY)),
            dma((NX,)),
            dma((NX,)),
            dma((NZ,)),
            dma((NZ,)),
        ],
        compiler_params=pltpu.CompilerParams(collective_id=1, has_side_effects=True),
        name="combine_rows",
    )(own_part, parts, out_weight)


def local(
    queries, fresh_span_keys, fresh_span_values, context_keys, context_values, selected, out_weight
):
    q_all, span_keys, span_values, pair_k, pair_v, own_part = gather(
        selected, queries, fresh_span_keys, fresh_span_values, context_keys, context_values
    )
    parts = attend(
        selected, q_all, span_keys, span_values, context_keys, context_values, pair_k, pair_v
    )
    return combine(own_part, parts, out_weight)


def solution(mesh):
    return jax.shard_map(
        local,
        mesh=mesh,
        in_specs=(
            P("ctx", "head"),
            P("ctx", "head"),
            P("ctx", "head"),
            P("ctx", "head"),
            P("ctx", "head"),
            P(),
            P("head", "ctx"),
        ),
        out_specs=P("head", "ctx"),
        check_vma=False,
    )
```
